512 devices in a mesh: row: 32 (over y_lo, z), col: 16 (over y_hi, x, core).
Axes of the slice: x: 4, y: 8 (y_hi: 2, y_lo: 4; y = y_hi * 4 + y_lo), z: 8, core: 2. Of those that a mesh axis runs over, the one named last changes fastest.
Arguments:
- a_blocks: bfloat16 [32, 16, 4, 3, 256, 256], P('row', 'col'), may hold values from -0.15625 to 0.15625
- a_columns: int32 [32, 16, 4, 3], P('row', 'col'), may hold values from 0 to 3, as said below
- a_live: int32 [32, 16, 4], P('row', 'col'), may hold values from 1 to 3, as said below
- owner_map: int32 [16, 2], P('col'), may hold values from 0 to 31, as said below
- b_blocks: bfloat16 [32, 16, 4, 256, 512], P('row', 'col'), may hold values from -6 to 6
- b_columns: int32 [32, 16, 4, 2], P('row', 'col'), may hold values from 0 to 3, as said below
Outputs:
- product_window: bfloat16 [32, 16, 4, 256, 1024], P('row', 'col')
The draws below stay inside these ranges and needn't reach their ends.
Inputs may be any that keep to these rules, and one draw needn't show every extreme that they name: `a_columns`: the 3 inner indices in a block row of an A tile differ. `a_live`: every A tile has a block row with 3 live slots. `owner_map`: the two grid rows named for a grid column differ. `b_columns`: the 2 block columns in a row of a B tile differ.
All inputs are finite; a program needn't handle non-finite values.
Results may differ from the reference program's by a relative error of at most 0.001.
Values may be sent and summed in bfloat16 or wider, within the bound.
No kernel may reach another device: no remote copies, remote signals or barrier semaphores. Data moves between devices by JAX's collectives and lax.ppermute only.
A program may use at most 64 MiB of HBM per device.

```python
import jax
import jax.numpy as jnp
from jax import lax

BS = 256
MB = 4
NZA = 3
KB = 4
NZB = 2
NB = 4
N_ROW = 32
N_COL = 16


def distinct_picks(key, leading, pool_size, picks):
    scores = jax.random.randint(key, leading + (pool_size,), 0, 1 << 20) * pool_size + jnp.arange(pool_size, dtype=jnp.int32)
    ordered = jnp.argsort(scores, axis=-1, stable=True)
    return ordered[..., :picks].astype(jnp.int32)


def draw_a_columns(key, part):
    return distinct_picks(key, (N_ROW, N_COL, MB), KB, NZA)


def draw_b_columns(key, part):
    return distinct_picks(key, (N_ROW, N_COL, KB), NB, NZB)


def draw_owner_map(key, part):
    pick_key = jax.random.fold_in(key, 11)
    column_key = jax.random.fold_in(key, 12)
    order_key = jax.random.fold_in(key, 13)
    picks = distinct_picks(pick_key, (N_COL,), N_ROW, 2)
    chosen = jax.random.randint(column_key, (), 0, N_COL)
    flipped = jax.random.randint(order_key, (), 0, 2)
    ends = jnp.array([0, N_ROW - 1], dtype=jnp.int32)
    pair = jnp.where(flipped == 0, ends, ends[::-1])
    at_chosen = jnp.arange(N_COL, dtype=jnp.int32)[:, None] == chosen
    return jnp.where(at_chosen, pair[None, :], picks).astype(jnp.int32)


def draw_a_live(key, part):
    first_key, second_key = jax.random.split(key)
    counts = jax.random.randint(first_key, (N_ROW, N_COL, MB), 1, NZA + 1)
    chosen = jax.random.randint(second_key, (N_ROW, N_COL, 1), 0, MB)
    full_row = jnp.arange(MB, dtype=jnp.int32)[None, None, :] == chosen
    return jnp.where(full_row, NZA, counts).astype(jnp.int32)


def block_levels(stream_key, dims, cuts, smallest, largest):
    factor_of = 1.0
    for dim, shards_of in cuts:
        draws = jax.random.uniform(jax.random.fold_in(jax.random.fold_in(stream_key, 6), dim), (shards_of,), jnp.float32, smallest / len(cuts), largest / len(cuts))
        factor_of = factor_of * jnp.repeat(jnp.exp(draws), dims[dim] // shards_of).reshape((-1,) + (1,) * (len(dims) - 1 - dim))
    return factor_of


def gaussian(stream_key, dims, width, most, shards=(), held_as=jnp.bfloat16):
    result = width * jax.random.normal(stream_key, dims, jnp.float32)
    if shards:
        result = result * block_levels(stream_key, dims, shards, -0.22, 0.18)
    return jnp.clip(result, -most, most).astype(held_as)


def setup_inputs(seed: int = 0) -> dict:
    keys = jax.random.split(jax.random.key(seed), 7)
    return {
        "a_blocks": gaussian(keys[0], (N_ROW, N_COL, MB, NZA, BS, BS), (2 * NZA * BS) ** -0.5, 0.15625, ((0, 32), (1, 16))),
        "a_columns": draw_a_columns(jax.random.fold_in(keys[6], 71), 0),
        "a_live": draw_a_live(jax.random.fold_in(keys[6], 71), 0),
        "owner_map": draw_owner_map(jax.random.fold_in(keys[6], 71), 0),
        "b_blocks": gaussian(keys[4], (N_ROW, N_COL, KB, BS, NZB * BS), 1.0, 6.0, ((0, 32), (1, 16))),
        "b_columns": draw_b_columns(jax.random.fold_in(keys[6], 71), 0),
    }


def section_term(blocks, columns, live_count, b_rows, b_targets):
    slot_index = jnp.arange(NZA, dtype=jnp.int32)
    live_mask = slot_index[None, :] < live_count[:, None]
    masked = jnp.where(live_mask[:, :, None, None], blocks, jnp.zeros_like(blocks))
    picked = b_rows[columns]
    partial_products = jnp.einsum("iaxy,iayw->iaxw", masked.astype(jnp.float32), picked.astype(jnp.float32))
    targets = b_targets[columns]
    select = (targets[..., None] == jnp.arange(NB, dtype=jnp.int32)).astype(jnp.float32)
    shaped = partial_products.reshape(MB, NZA, BS, NZB, BS)
    placed = jnp.einsum("iaxtz,iatj->ixjz", shaped, select, precision=lax.Precision.HIGHEST)
    return placed.reshape(MB, BS, NB * BS)


def reference(a_blocks, a_columns, a_live, owner_map, b_blocks, b_columns):
    def one_cell(cell_index):
        cell_row = cell_index // N_COL
        cell_col = cell_index % N_COL
        summed = jnp.zeros((MB, BS, NB * BS), jnp.float32)
        for offset in (0, 1):
            holder = owner_map[cell_col, offset]
            source = (cell_col + offset) % N_COL
            summed = summed + section_term(a_blocks[holder, cell_col], a_columns[holder, cell_col], a_live[holder, cell_col], b_blocks[cell_row, source], b_columns[cell_row, source])
        return summed.astype(jnp.bfloat16)

    cells = lax.map(one_cell, jnp.arange(N_ROW * N_COL, dtype=jnp.int32))
    return cells.reshape(N_ROW, N_COL, MB, BS, NB * BS)
```

```python
import jax
import jax.numpy as jnp
from jax import lax
from jax.experimental import pallas as pl
from jax.experimental.pallas import tpu as pltpu
from jax.sharding import Mesh, PartitionSpec as P

BS = 256
MB = 4
NZA = 3
KB = 4
NZB = 2
NB = 4
Y_LO = 4
Z = 8
COL = ("y_hi", "x", "core")
ROW = ("y_lo", "z")
PIECES = Y_LO * Z
PIECE = MB * NZA * BS // PIECES
SPAN = Y_LO * PIECE
META = 8


def z_route(distance):
    return [(i, (i + distance) % Z) for i in range(Z)]


def col_route(n):
    return [((i + 1) % n, i) for i in range(n)]


def products(ints, own, f1, b1, f2, b2, f3, b3, f4, b4, b_here, b_next, out, a_s, b_s, acc, sem):
    i = pl.program_id(0)

    @pl.when(i == 0)
    def _():
        z = ints[0]
        copies = []
        for n, (ref, away) in enumerate(((own, 0), (f1, -1), (b1, 1), (f2, -2), (b2, 2), (f3, -3), (b3, 3))):
            start = pl.multiple_of(((z + Z + away) % Z) * SPAN, SPAN)
            copies.append(pltpu.make_async_copy(ref, a_s.at[:, pl.ds(start, SPAN)], sem.at[n]))
        start = pl.multiple_of(((z + 4) % Z) * SPAN, SPAN)
        half = SPAN // 2
        copies.append(pltpu.make_async_copy(f4, a_s.at[:, pl.ds(start, half)], sem.at[7]))
        copies.append(pltpu.make_async_copy(b4, a_s.at[:, pl.ds(pl.multiple_of(start + half, half), half)], sem.at[8]))
        copies.append(pltpu.make_async_copy(b_here, b_s.at[0], sem.at[9]))
        copies.append(pltpu.make_async_copy(b_next, b_s.at[1], sem.at[10]))
        for c in copies:
            c.start()
        for c in copies:
            c.wait()

    acc[...] = jnp.zeros_like(acc)
    for k in range(2):
        for s in range(NZA):
            at = 1 + k * 24 + i * NZA + s
            live = ints[1 + k * 24 + 12 + i]

            @pl.when(s < live)
            def _():
                q = ints[at]
                row = pl.multiple_of((i * NZA + s) * BS, BS)
                product = jnp.dot(a_s[k, pl.ds(row, BS), :], b_s[k, q], preferred_element_type=jnp.float32)
                for t in range(NZB):
                    j = ints[1 + k * 24 + 16 + q * NZB + t]
                    acc[j] += product[:, t * BS : (t + 1) * BS]

    for j in range(NB):
        out[0, :, j * BS : (j + 1) * BS] = acc[j].astype(jnp.bfloat16)


def on_device(a_blocks, a_columns, a_live, owner_map, b_blocks, b_columns):
    tile = a_blocks.reshape(PIECES, PIECE, BS)
    meta = jnp.concatenate([a_columns.reshape(-1), a_live.reshape(-1)]).astype(jnp.bfloat16)
    meta = jnp.pad(meta[None, :], ((0, META - 1), (0, BS - meta.shape[0])))
    sent = jnp.concatenate([tile, jnp.broadcast_to(meta[None], (PIECES, META, BS))], axis=1)
    got = lax.all_to_all(sent, ("z", "y_lo"), 0, 0, tiled=True)
    holder = owner_map[0]
    source = (holder % Z) * Y_LO + holder // Z
    two = jnp.stack([lax.dynamic_index_in_dim(got, source[k], 0, keepdims=False) for k in range(2)])
    mine = two[:, :PIECE]
    own = lax.all_gather(mine, "y_lo", axis=1, tiled=True)

    b_here = b_blocks[0, 0]
    cols = lax.axis_size(COL)
    b_ready, own = lax.optimization_barrier((b_here, own))
    b_next = lax.ppermute(b_ready, COL, col_route(cols))
    bc_next = lax.ppermute(b_columns[0, 0], COL, col_route(cols))

    ahead = [own]
    back = [own]
    for _ in range(3):
        ahead.append(lax.ppermute(ahead[-1], "z", z_route(1)))
        back.append(lax.ppermute(back[-1], "z", z_route(-1)))
    f4 = lax.ppermute(ahead[3][:, : SPAN // 2], "z", z_route(1))
    b4 = lax.ppermute(back[3][:, SPAN // 2 :], "z", z_route(-1))

    pairs = [b_columns[0, 0].reshape(-1), bc_next.reshape(-1)]
    ints = [lax.axis_index("z").astype(jnp.int32)[None]]
    for k in range(2):
        ints += [two[k, PIECE, : MB * NZA + MB].astype(jnp.int32), pairs[k]]
    ints = jnp.concatenate(ints)

    hbm = pl.BlockSpec(memory_space=pl.ANY)
    window = pl.pallas_call(
        products,
        out_shape=jax.ShapeDtypeStruct((MB, BS, NB * BS), jnp.bfloat16),
        grid_spec=pltpu.PrefetchScalarGridSpec(
            num_scalar_prefetch=1,
            grid=(MB,),
            in_specs=[hbm] * 11,
            out_specs=pl.BlockSpec((1, BS, NB * BS), lambda i, ints: (i, 0, 0)),
            scratch_shapes=[
                pltpu.VMEM((2, MB * NZA * BS, BS), jnp.bfloat16),
                pltpu.VMEM((2, KB, BS, NZB * BS), jnp.bfloat16),
                pltpu.VMEM((NB, BS, BS), jnp.float32),
                pltpu.SemaphoreType.DMA((11,)),
            ],
        ),
        compiler_params=pltpu.CompilerParams(vmem_limit_bytes=24 * 1024 * 1024),
    )(ints, own, ahead[1], back[1], ahead[2], back[2], ahead[3], back[3], f4, b4, b_here, b_next)
    return window[None, None]


def solution(mesh):
    fine = Mesh(mesh.devices.reshape(Y_LO, Z, 2, 4, 2), ROW + COL)
    row, col = ROW, COL
    return jax.shard_map(
        on_device,
        mesh=fine,
        in_specs=(
            P(row, col, None, None, None, None),
            P(row, col, None, None),
            P(row, col, None),
            P(col, None),
            P(row, col, None, None, None),
            P(row, col, None, None),
        ),
        out_specs=P(row, col, None, None, None),
        check_vma=False,
    )
```

```python
import jax
import jax.numpy as jnp
from jax import lax
from jax.experimental import pallas as pl
from jax.experimental.pallas import tpu as pltpu
from jax.sharding import Mesh, PartitionSpec as P

BS = 256
MB = 4
NZA = 3
KB = 4
NZB = 2
NB = 4
Y_LO = 4
Z = 8
COL = ("y_hi", "x", "core")
ROW = ("y_lo", "z")
PIECES = Y_LO * Z
PIECE = MB * NZA * BS // PIECES
SPAN = Y_LO * PIECE


def z_route(distance):
    return [(i, (i + distance) % Z) for i in range(Z)]


def col_route(n):
    return [((i + 1) % n, i) for i in range(n)]


def products(ints, own, f1, b1, f2, b2, f3, b3, f4, b4, b_here, b_next, out, a_s, b_s, acc, sem):
    i = pl.program_id(0)

    @pl.when(i == 0)
    def _():
        z = ints[0]
        copies = []
        for n, (ref, away) in enumerate(((own, 0), (f1, -1), (b1, 1), (f2, -2), (b2, 2), (f3, -3), (b3, 3))):
            start = pl.multiple_of(((z + Z + away) % Z) * SPAN, SPAN)
            copies.append(pltpu.make_async_copy(ref, a_s.at[:, pl.ds(start, SPAN)], sem.at[n]))
        start = pl.multiple_of(((z + 4) % Z) * SPAN, SPAN)
        half = SPAN // 2
        copies.append(pltpu.make_async_copy(f4, a_s.at[:, pl.ds(start, half)], sem.at[7]))
        copies.append(pltpu.make_async_copy(b4, a_s.at[:, pl.ds(pl.multiple_of(start + half, half), half)], sem.at[8]))
        copies.append(pltpu.make_async_copy(b_here, b_s.at[0], sem.at[9]))
        copies.append(pltpu.make_async_copy(b_next, b_s.at[1], sem.at[10]))
        for c in copies:
            c.start()
        for c in copies:
            c.wait()

    acc[...] = jnp.zeros_like(acc)
    for k in range(2):
        for s in range(NZA):
            at = 1 + k * 24 + i * NZA + s
            live = ints[1 + k * 24 + 12 + i]

            @pl.when(s < live)
            def _():
                q = ints[at]
                row = pl.multiple_of((i * NZA + s) * BS, BS)
                product = jnp.dot(a_s[k, pl.ds(row, BS), :], b_s[k, q], preferred_element_type=jnp.float32)
                for t in range(NZB):
                    j = ints[1 + k * 24 + 16 + q * NZB + t]
                    acc[j] += product[:, t * BS : (t + 1) * BS]

    for j in range(NB):
        out[0, :, j * BS : (j + 1) * BS] = acc[j].astype(jnp.bfloat16)


def shared_ints(a_columns, a_live, holder, b_columns, cols):
    mine = jnp.concatenate([a_columns.reshape(-1), a_live.reshape(-1)])
    here = lax.axis_index(ROW) == holder
    table = jnp.where(here[:, None], mine[None, :], 0).reshape(1, -1)
    table = jnp.pad(table, ((0, 0), (0, 128 - table.shape[1])))
    for axis, bit in (("y_lo", 1), ("y_lo", 2), ("z", 1), ("z", 2), ("z", 4)):
        table = table + lax.ppermute(table, axis, [(i, i ^ bit) for i in range(lax.axis_size(axis))])
    bc_here = b_columns[0, 0]
    bc_next = lax.ppermute(bc_here, COL, col_route(cols))
    each = MB * NZA + MB
    return jnp.concatenate(
        [
            lax.axis_index("z").astype(jnp.int32)[None],
            table[0, :each],
            bc_here.reshape(-1),
            table[0, each : 2 * each],
            bc_next.reshape(-1),
        ]
    )


def on_device(a_blocks, a_columns, a_live, owner_map, b_blocks, b_columns):
    tile = a_blocks.reshape(PIECES, PIECE, BS)
    cols = lax.axis_size(COL)
    got = lax.all_to_all(tile, ("z", "y_lo"), 0, 0, tiled=True)
    holder = owner_map[0]
    source = (holder % Z) * Y_LO + holder // Z
    ints = shared_ints(a_columns, a_live, holder, b_columns, cols)
    got, ints = lax.optimization_barrier((got, ints))
    mine = jnp.stack([lax.dynamic_index_in_dim(got, source[k], 0, keepdims=False) for k in range(2)])
    own = lax.all_gather(mine, "y_lo", axis=1, tiled=True)

    b_here = b_blocks[0, 0]
    b_ready, own = lax.optimization_barrier((b_here, own))
    b_next = lax.ppermute(b_ready, COL, col_route(cols))

    ahead = [own]
    back = [own]
    for _ in range(3):
        ahead.append(lax.ppermute(ahead[-1], "z", z_route(1)))
        back.append(lax.ppermute(back[-1], "z", z_route(-1)))
    f4 = lax.ppermute(ahead[3][:, : SPAN // 2], "z", z_route(1))
    b4 = lax.ppermute(back[3][:, SPAN // 2 :], "z", z_route(-1))

    hbm = pl.BlockSpec(memory_space=pl.ANY)
    window = pl.pallas_call(
        products,
        out_shape=jax.ShapeDtypeStruct((MB, BS, NB * BS), jnp.bfloat16),
        grid_spec=pltpu.PrefetchScalarGridSpec(
            num_scalar_prefetch=1,
            grid=(MB,),
            in_specs=[hbm] * 11,
            out_specs=pl.BlockSpec((1, BS, NB * BS), lambda i, ints: (i, 0, 0)),
            scratch_shapes=[
                pltpu.VMEM((2, MB * NZA * BS, BS), jnp.bfloat16),
                pltpu.VMEM((2, KB, BS, NZB * BS), jnp.bfloat16),
                pltpu.VMEM((NB, BS, BS), jnp.float32),
                pltpu.SemaphoreType.DMA((11,)),
            ],
        ),
        compiler_params=pltpu.CompilerParams(vmem_limit_bytes=24 * 1024 * 1024),
    )(ints, own, ahead[1], back[1], ahead[2], back[2], ahead[3], back[3], f4, b4, b_here, b_next)
    return window[None, None]


def solution(mesh):
    fine = Mesh(mesh.devices.reshape(Y_LO, Z, 2, 4, 2), ROW + COL)
    row, col = ROW, COL
    return jax.shard_map(
        on_device,
        mesh=fine,
        in_specs=(
            P(row, col, None, None, None, None),
            P(row, col, None, None),
            P(row, col, None),
            P(col, None),
            P(row, col, None, None, None),
            P(row, col, None, None),
        ),
        out_specs=P(row, col, None, None, None),
        check_vma=False,
    )
```

```python
import jax
import jax.numpy as jnp
from jax import lax
from jax.experimental import pallas as pl
from jax.experimental.pallas import tpu as pltpu
from jax.sharding import Mesh, PartitionSpec as P

BS = 256
MB = 4
NZA = 3
KB = 4
NZB = 2
NB = 4
Y_LO = 4
Z = 8
COL = ("y_hi", "x", "core")
ROW = ("y_lo", "z")
PIECES = Y_LO * Z
PIECE = MB * NZA * BS // PIECES
SPAN = Y_LO * PIECE


def z_route(distance):
    return [(i, (i + distance) % Z) for i in range(Z)]


def col_route(n):
    return [((i + 1) % n, i) for i in range(n)]


def block_rows(rounds, ints, refs, b_refs, out, a_s, o_s, acc, sem, osem):
    place, table, rest, b_columns = ints[0], ints[1], ints[2], ints[3:]
    z = place[0]
    copies = []
    for n, (ref, away, start, rows) in enumerate(refs):
        at = pl.multiple_of(((z + Z + away) % Z) * SPAN + start, SPAN // 2)
        copies.append(pltpu.make_async_copy(ref, a_s.at[:, pl.ds(at, rows)], sem.at[n]))
    for c in copies:
        c.start()
    for c in copies:
        c.wait()
    odd = z % 2
    writes = []
    for n, even_row, odd_row in rounds:
        i = ((z + even_row + odd * (odd_row - even_row) + Z) % Z) // 2
        acc[...] = jnp.zeros_like(acc)
        for k in range(2):
            for s in range(NZA):
                base = k * EACH
                live = table[0, base + MB * NZA + i] + rest[0, base + MB * NZA + i]

                @pl.when(s < live)
                def _():
                    at = base + i * NZA + s
                    q = table[0, at] + rest[0, at]
                    row = pl.multiple_of((i * NZA + s) * BS, BS)
                    product = jnp.dot(a_s[k, pl.ds(row, BS), :], b_refs[k][q], preferred_element_type=jnp.float32)
                    for t in range(NZB):
                        j = b_columns[k][q * NZB + t]
                        acc[j] += product[:, t * BS : (t + 1) * BS]

        for j in range(NB):
            o_s[n, :, j * BS : (j + 1) * BS] = acc[j].astype(jnp.bfloat16)
        writes.append(pltpu.make_async_copy(o_s.at[n], out.at[i], osem.at[n]))
        writes[-1].start()
    for w in writes:
        w.wait()


def two_rows(place, table, rest, bc_here, bc_next, own, f1, b1, f2, b2, b_here, b_next, out, *scratch):
    refs = [(own, 0, 0, SPAN), (f1, -1, 0, SPAN), (b1, 1, 0, SPAN), (f2, -2, 0, SPAN), (b2, 2, 0, SPAN)]
    block_rows([(0, 0, 0), (1, -2, 1)], (place, table, rest, bc_here, bc_next), refs, (b_here, b_next), out, *scratch)


def third_row(place, table, rest, bc_here, bc_next, f2, b2, f3, b3, b_here, b_next, before, out, *scratch):
    refs = [(f2, -2, 0, SPAN), (b2, 2, 0, SPAN), (f3, -3, 0, SPAN), (b3, 3, 0, SPAN)]
    block_rows([(0, 2, -3)], (place, table, rest, bc_here, bc_next), refs, (b_here, b_next), out, *scratch)


def last_row(place, table, rest, bc_here, bc_next, f3, b3, f4, b4, b_here, b_next, before, out, *scratch):
    half = SPAN // 2
    refs = [(f3, -3, 0, SPAN), (b3, 3, 0, SPAN), (f4, 4, 0, half), (b4, 4, half, half)]
    block_rows([(0, 4, 3)], (place, table, rest, bc_here, bc_next), refs, (b_here, b_next), out, *scratch)


def call(kernel, rows, ints, pieces, b_pair, before):
    hbm = pl.BlockSpec(memory_space=pl.ANY)
    vmem = pl.BlockSpec(memory_space=pltpu.VMEM)
    ends = [] if before is None else [before]
    return pl.pallas_call(
        kernel,
        out_shape=jax.ShapeDtypeStruct((MB, BS, NB * BS), jnp.bfloat16),
        grid_spec=pltpu.PrefetchScalarGridSpec(
            num_scalar_prefetch=len(ints),
            grid=(),
            in_specs=[hbm] * len(pieces) + [vmem] * 2 + [hbm] * len(ends),
            out_specs=hbm,
            scratch_shapes=[
                pltpu.VMEM((2, MB * NZA * BS, BS), jnp.bfloat16),
                pltpu.VMEM((rows, BS, NB * BS), jnp.bfloat16),
                pltpu.VMEM((NB, BS, BS), jnp.float32),
                pltpu.SemaphoreType.DMA((len(pieces),)),
                pltpu.SemaphoreType.DMA((rows,)),
            ],
        ),
        input_output_aliases={len(ints) + len(pieces) + 2: 0} if ends else {},
        cost_estimate=pl.CostEstimate(flops=rows * 12 * BS**3 * 2, bytes_accessed=rows << 20, transcendentals=0),
        compiler_params=pltpu.CompilerParams(vmem_limit_bytes=12 * 1024 * 1024),
    )(*ints, *pieces, *b_pair, *ends)


EACH = MB * NZA + MB


def masked_ints(a_columns, a_live, holder):
    mine = jnp.concatenate([a_columns.reshape(-1), a_live.reshape(-1)])
    here = lax.axis_index(ROW) == holder
    table = jnp.where(here[:, None], mine[None, :], 0).reshape(1, -1)
    table = jnp.pad(table, ((0, 0), (0, 128 - table.shape[1])))
    total = table
    for distance in range(1, Z):
        total = total + lax.ppermute(table, "z", z_route(distance))
    return total


def on_device(a_blocks, a_columns, a_live, owner_map, b_blocks, b_columns):
    tile = a_blocks.reshape(PIECES, PIECE, BS)
    cols = lax.axis_size(COL)
    got = lax.all_to_all(tile, ("z", "y_lo"), 0, 0, tiled=True)
    holder = owner_map[0]
    source = (holder % Z) * Y_LO + holder // Z
    table = masked_ints(a_columns, a_live, holder)
    bc_here = b_columns[0, 0]
    bc_next = lax.ppermute(bc_here, COL, col_route(cols)).reshape(-1)
    bc_here = bc_here.reshape(-1)
    got, table, bc_here, bc_next = lax.optimization_barrier((got, table, bc_here, bc_next))

    first = lax.ppermute(table, "y_lo", [(i, i ^ 1) for i in range(Y_LO)])
    two = jnp.stack([lax.dynamic_index_in_dim(got, source[k], 0, keepdims=False) for k in range(2)])
    own = lax.all_gather(two, "y_lo", axis=1, tiled=True)
    own, first = lax.optimization_barrier((own, first))
    b_here = b_blocks[0, 0]
    b_ready, own, table = lax.optimization_barrier((b_here, own, table + first))
    b_next = lax.ppermute(b_ready, COL, col_route(cols))
    rest = lax.ppermute(table, "y_lo", [(i, i ^ 2) for i in range(Y_LO)])
    ahead = [own]
    back = [own]
    for step in range(3):
        ahead.append(lax.ppermute(ahead[-1], "z", z_route(1)))
        back.append(lax.ppermute(back[-1], "z", z_route(-1)))
        if step == 1:
            ahead[2], back[2], rest = lax.optimization_barrier((ahead[2], back[2], rest))
    f4 = lax.ppermute(ahead[3][:, : SPAN // 2], "z", z_route(1))
    b4 = lax.ppermute(back[3][:, SPAN // 2 :], "z", z_route(-1))

    b_pair = (b_here, b_next)
    ints = (lax.axis_index("z").astype(jnp.int32)[None], table, rest, bc_here, bc_next)
    window = call(two_rows, 2, ints, (own, ahead[1], back[1], ahead[2], back[2]), b_pair, None)
    window = call(third_row, 1, ints, (ahead[2], back[2], ahead[3], back[3]), b_pair, window)
    window = call(last_row, 1, ints, (ahead[3], back[3], f4, b4), b_pair, window)
    return window[None, None]


def solution(mesh):
    fine = Mesh(mesh.devices.reshape(Y_LO, Z, 2, 4, 2), ROW + COL)
    row, col = ROW, COL
    return jax.shard_map(
        on_device,
        mesh=fine,
        in_specs=(
            P(row, col, None, None, None, None),
            P(row, col, None, None),
            P(row, col, None),
            P(col, None),
            P(row, col, None, None, None),
            P(row, col, None, None),
        ),
        out_specs=P(row, col, None, None, None),
        check_vma=False,
    )
```

```python
import jax
import jax.numpy as jnp
from jax import lax
from jax.experimental import pallas as pl
from jax.experimental.pallas import tpu as pltpu
from jax.sharding import Mesh, PartitionSpec as P

BS = 256
MB = 4
NZA = 3
KB = 4
NZB = 2
NB = 4
Y_LO = 4
Z = 8
COL = ("y_hi", "x", "core")
ROW = ("y_lo", "z")
PIECES = Y_LO * Z
PIECE = MB * NZA * BS // PIECES
SPAN = Y_LO * PIECE
META = 8


def z_route(distance):
    return [(i, (i + distance) % Z) for i in range(Z)]


def col_route(n):
    return [((i + 1) % n, i) for i in range(n)]


def block_rows(rounds, ints, refs, b_refs, out, a_s, o_s, acc, sem, osem):
    place, table, b_columns = ints[0], ints[1], ints[2:]
    z = place[0]
    copies = []
    for n, (ref, away, start, rows) in enumerate(refs):
        at = pl.multiple_of(((z + Z + away) % Z) * SPAN + start, SPAN // 2)
        copies.append(pltpu.make_async_copy(ref, a_s.at[:, pl.ds(at, rows)], sem.at[n]))
    for c in copies:
        c.start()
    for c in copies:
        c.wait()
    odd = z % 2
    writes = []
    for n, even_row, odd_row in rounds:
        i = ((z + even_row + odd * (odd_row - even_row) + Z) % Z) // 2
        acc[...] = jnp.zeros_like(acc)
        for k in range(2):
            for s in range(NZA):
                base = k * EACH
                live = table[base + MB * NZA + i]

                @pl.when(s < live)
                def _():
                    q = table[base + i * NZA + s]
                    row = pl.multiple_of((i * NZA + s) * BS, BS)
                    product = jnp.dot(a_s[k, pl.ds(row, BS), :], b_refs[k][q], preferred_element_type=jnp.float32)
                    for t in range(NZB):
                        j = b_columns[k][q * NZB + t]
                        acc[j] += product[:, t * BS : (t + 1) * BS]

        for j in range(NB):
            o_s[n, :, j * BS : (j + 1) * BS] = acc[j].astype(jnp.bfloat16)
        writes.append(pltpu.make_async_copy(o_s.at[n], out.at[i], osem.at[n]))
        writes[-1].start()
    for w in writes:
        w.wait()


def two_rows(place, table, bc_here, bc_next, own, f1, b1, f2, b2, b_here, b_next, out, *scratch):
    refs = [(own, 0, 0, SPAN), (f1, -1, 0, SPAN), (b1, 1, 0, SPAN), (f2, -2, 0, SPAN), (b2, 2, 0, SPAN)]
    block_rows([(0, 0, 0), (1, -2, 1)], (place, table, bc_here, bc_next), refs, (b_here, b_next), out, *scratch)


def third_row(place, table, bc_here, bc_next, f2, b2, f3, b3, b_here, b_next, before, out, *scratch):
    refs = [(f2, -2, 0, SPAN), (b2, 2, 0, SPAN), (f3, -3, 0, SPAN), (b3, 3, 0, SPAN)]
    block_rows([(0, 2, -3)], (place, table, bc_here, bc_next), refs, (b_here, b_next), out, *scratch)


def last_row(place, table, bc_here, bc_next, f3, b3, f4, b4, b_here, b_next, before, out, *scratch):
    half = SPAN // 2
    refs = [(f3, -3, 0, SPAN), (b3, 3, 0, SPAN), (f4, 4, 0, half), (b4, 4, half, half)]
    block_rows([(0, 4, 3)], (place, table, bc_here, bc_next), refs, (b_here, b_next), out, *scratch)


def call(kernel, rows, ints, pieces, b_pair, before):
    hbm = pl.BlockSpec(memory_space=pl.ANY)
    vmem = pl.BlockSpec(memory_space=pltpu.VMEM)
    ends = [] if before is None else [before]
    return pl.pallas_call(
        kernel,
        out_shape=jax.ShapeDtypeStruct((MB, BS, NB * BS), jnp.bfloat16),
        grid_spec=pltpu.PrefetchScalarGridSpec(
            num_scalar_prefetch=len(ints),
            grid=(),
            in_specs=[hbm] * len(pieces) + [vmem] * 2 + [hbm] * len(ends),
            out_specs=hbm,
            scratch_shapes=[
                pltpu.VMEM((2, MB * NZA * BS, BS), jnp.bfloat16),
                pltpu.VMEM((rows, BS, NB * BS), jnp.bfloat16),
                pltpu.VMEM((NB, BS, BS), jnp.float32),
                pltpu.SemaphoreType.DMA((len(pieces),)),
                pltpu.SemaphoreType.DMA((rows,)),
            ],
        ),
        input_output_aliases={len(ints) + len(pieces) + 2: 0} if ends else {},
        cost_estimate=pl.CostEstimate(flops=rows * 12 * BS**3 * 2, bytes_accessed=rows << 20, transcendentals=0),
        compiler_params=pltpu.CompilerParams(vmem_limit_bytes=12 * 1024 * 1024),
    )(*ints, *pieces, *b_pair, *ends)


EACH = MB * NZA + MB


def payload_rows(a_columns, a_live, tile, out, rows, sem):
    copy = pltpu.make_async_copy(tile, out.at[:, :PIECE], sem.at[0])
    copy.start()
    lane = lax.broadcasted_iota(jnp.int32, (META, BS), 1)
    row = jnp.zeros((META, BS), jnp.int32)
    for i in range(MB):
        for s in range(NZA):
            row = jnp.where(lane == i * NZA + s, a_columns[i, s], row)
        row = jnp.where(lane == MB * NZA + i, a_live[i], row)
    rows[...] = jnp.broadcast_to(row.astype(jnp.float32).astype(jnp.bfloat16)[None], rows.shape)
    below = pltpu.make_async_copy(rows, out.at[:, PIECE:], sem.at[1])
    below.start()
    copy.wait()
    below.wait()


def payload(a_columns, a_live, tile):
    return pl.pallas_call(
        payload_rows,
        out_shape=jax.ShapeDtypeStruct((PIECES, PIECE + META, BS), jnp.bfloat16),
        grid_spec=pltpu.PrefetchScalarGridSpec(
            num_scalar_prefetch=2,
            grid=(),
            in_specs=[pl.BlockSpec(memory_space=pltpu.HBM)],
            out_specs=pl.BlockSpec(memory_space=pl.ANY),
            scratch_shapes=[
                pltpu.VMEM((PIECES, META, BS), jnp.bfloat16),
                pltpu.SemaphoreType.DMA((2,)),
            ],
        ),
        compiler_params=pltpu.CompilerParams(vmem_limit_bytes=4 * 1024 * 1024),
    )(a_columns, a_live, tile)


def on_device(a_blocks, a_columns, a_live, owner_map, b_blocks, b_columns):
    tile = a_blocks.reshape(PIECES, PIECE, BS)
    cols = lax.axis_size(COL)
    got = lax.all_to_all(payload(a_columns[0, 0], a_live[0, 0], tile), ("z", "y_lo"), 0, 0, tiled=True)
    holder = owner_map[0]
    source = (holder % Z) * Y_LO + holder // Z
    bc_here = b_columns[0, 0]
    bc_next = lax.ppermute(bc_here, COL, col_route(cols)).reshape(-1)
    bc_here = bc_here.reshape(-1)
    place = lax.axis_index("z").astype(jnp.int32)[None]
    got, bc_here, bc_next, place = lax.optimization_barrier((got, bc_here, bc_next, place))

    two = jnp.stack([lax.dynamic_index_in_dim(got, source[k], 0, keepdims=False) for k in range(2)])
    table = two[:, PIECE, :EACH].astype(jnp.int32).reshape(-1)
    own = lax.all_gather(two[:, :PIECE], "y_lo", axis=1, tiled=True)
    b_here = b_blocks[0, 0]
    b_ready, own, table = lax.optimization_barrier((b_here, own, table))
    b_next = lax.ppermute(b_ready, COL, col_route(cols))
    ahead = [own]
    back = [own]
    for step in range(3):
        ahead.append(lax.ppermute(ahead[-1], "z", z_route(1)))
        back.append(lax.ppermute(back[-1], "z", z_route(-1)))
    b_pair = (b_here, b_next)
    ints = (place, table, bc_here, bc_next)
    window = call(two_rows, 2, ints, (own, ahead[1], back[1], ahead[2], back[2]), b_pair, None)
    window, ahead[3], back[3] = lax.optimization_barrier((window, ahead[3], back[3]))
    f4 = lax.ppermute(ahead[3][:, : SPAN // 2], "z", z_route(1))
    b4 = lax.ppermute(back[3][:, SPAN // 2 :], "z", z_route(-1))
    window = call(third_row, 1, ints, (ahead[2], back[2], ahead[3], back[3]), b_pair, window)
    window = call(last_row, 1, ints, (ahead[3], back[3], f4, b4), b_pair, window)
    return window[None, None]


def solution(mesh):
    fine = Mesh(mesh.devices.reshape(Y_LO, Z, 2, 4, 2), ROW + COL)
    row, col = ROW, COL
    return jax.shard_map(
        on_device,
        mesh=fine,
        in_specs=(
            P(row, col, None, None, None, None),
            P(row, col, None, None),
            P(row, col, None),
            P(col, None),
            P(row, col, None, None, None),
            P(row, col, None, None),
        ),
        out_specs=P(row, col, None, None, None),
        check_vma=False,
    )
```

```python
import jax
import jax.numpy as jnp
from jax import lax
from jax.experimental import pallas as pl
from jax.experimental.pallas import tpu as pltpu
from jax.sharding import Mesh, PartitionSpec as P

BS = 256
MB = 4
NZA = 3
KB = 4
NZB = 2
NB = 4
Y_LO = 4
Z = 8
COL = ("y_hi", "x", "core")
ROW = ("y_lo", "z")
PIECES = Y_LO * Z
PIECE = MB * NZA * BS // PIECES
SPAN = Y_LO * PIECE
META = 8


def z_route(distance):
    return [(i, (i + distance) % Z) for i in range(Z)]


def col_route(n):
    return [((i + 1) % n, i) for i in range(n)]


EACH = MB * NZA + MB


def strips(parts):
    found = []
    at = 0
    for ref in parts:
        rows = ref.shape[1]
        off = 0
        while off < rows:
            slot = at // BS
            take = min(rows - off, (slot + 1) * BS - at)
            found.append((slot, at - slot * BS, ref, off, take))
            off += take
            at += take
    return found


def add_products(scalars, i, k, parts, b_ref, acc):
    table, pairs = scalars[1], scalars[2 + k]
    live = table[k * EACH + MB * NZA + i]
    for s in range(NZA):

        @pl.when(s < live)
        def _():
            q = table[k * EACH + i * NZA + s]
            b = b_ref[q]
            for slot, row, ref, off, take in strips(parts):
                if slot == s:
                    product = jnp.dot(ref[k, off : off + take, :], b, preferred_element_type=jnp.float32)
                    for t in range(NZB):
                        j = pairs[q * NZB + t]
                        acc[j, row : row + take] += product[:, t * BS : (t + 1) * BS]


def on_parity(scalars, even, odd, sections, b_refs, acc):
    z = scalars[0][0]
    for bit, (away, parts) in enumerate((even, odd)):

        @pl.when(z % 2 == bit)
        def _():
            i = ((z + away + Z) % Z) // 2
            for k in sections:
                add_products(scalars, i, k, parts, b_refs[k], acc)

    return ((z + even[0] + (z % 2) * (odd[0] - even[0]) + Z) % Z) // 2


def write_row(o_s, acc, out, i, sem):
    for j in range(NB):
        o_s[:, j * BS : (j + 1) * BS] = acc[j].astype(jnp.bfloat16)
    copy = pltpu.make_async_copy(o_s, out.at[i], sem)
    copy.start()
    return copy


def first_section(*refs):
    scalars, (own, f1, b1, f2, b2, b_here, part, acc, sem) = refs[:4], refs[4:]
    acc[...] = jnp.zeros_like(acc)
    rows = (((0, (own, b1)), (-1, (f1, own))), ((-2, (f2, f1)), (1, (b1, b2))))
    copies = []
    for n, (even, odd) in enumerate(rows):
        on_parity(scalars, even, odd, (0,), (b_here,), acc.at[n])
        copies.append(pltpu.make_async_copy(acc.at[n], part.at[n], sem.at[n]))
        copies[-1].start()
    for c in copies:
        c.wait()


def three_rows(*refs):
    scalars = refs[:4]
    own, f1, b1, f2, b2, f3, b3, b_here, b_next, part, out, acc, o_s, sem = refs[4:]
    b_refs = (b_here, b_next)
    loads = [pltpu.make_async_copy(part.at[n], acc.at[n], sem.at[n]) for n in range(2)]
    for c in loads:
        c.start()
    acc[2] = jnp.zeros_like(acc[2])
    i = on_parity(scalars, (2, (b2, b3)), (-3, (f3, f2)), (0, 1), b_refs, acc.at[2])
    writes = [write_row(o_s.at[2], acc.at[2], out, i, sem.at[2])]
    rows = (((0, (own, b1)), (-1, (f1, own))), ((-2, (f2, f1)), (1, (b1, b2))))
    for n, (even, odd) in enumerate(rows):
        loads[n].wait()
        i = on_parity(scalars, even, odd, (1,), b_refs, acc.at[n])
        writes.append(write_row(o_s.at[n], acc.at[n], out, i, sem.at[3 + n]))
    for c in writes:
        c.wait()


def last_row(*refs):
    scalars = refs[:4]
    f3, b3, f4, b4, b_here, b_next, before, out, acc, o_s, sem = refs[4:]
    acc[...] = jnp.zeros_like(acc)
    i = on_parity(scalars, (4, (f4, b4, f3)), (3, (b3, f4, b4)), (0, 1), (b_here, b_next), acc)
    write_row(o_s, acc, out, i, sem.at[0]).wait()


def call(kernel, scalars, held, left, out_shape, scratch, products, alias=False):
    hbm = pl.BlockSpec(memory_space=pl.ANY)
    vmem = pl.BlockSpec(memory_space=pltpu.VMEM)
    return pl.pallas_call(
        kernel,
        out_shape=out_shape,
        grid_spec=pltpu.PrefetchScalarGridSpec(
            num_scalar_prefetch=len(scalars),
            grid=(),
            in_specs=[vmem] * len(held) + [hbm] * len(left),
            out_specs=hbm,
            scratch_shapes=scratch,
        ),
        input_output_aliases={len(scalars) + len(held): 0} if alias else {},
        cost_estimate=pl.CostEstimate(flops=products * 4 * BS**3, bytes_accessed=1 << 20, transcendentals=0),
        compiler_params=pltpu.CompilerParams(vmem_limit_bytes=12 * 1024 * 1024),
    )(*scalars, *held, *left)


def payload_rows(a_columns, a_live, tile, out, wide, rows, sem):
    copy = pltpu.make_async_copy(tile, out.at[:, :PIECE], sem.at[0])
    copy.start()
    wide[...] = jnp.zeros_like(wide)
    for i in range(MB):
        wide[:1, i * NZA : (i + 1) * NZA] = a_columns[i : i + 1].astype(jnp.float32)
    wide[:1, MB * NZA : EACH] = a_live[...].astype(jnp.float32)
    rows[...] = jnp.broadcast_to(wide[...].astype(jnp.bfloat16)[None], rows.shape)
    below = pltpu.make_async_copy(rows, out.at[:, PIECE:], sem.at[1])
    below.start()
    copy.wait()
    below.wait()


def payload(a_columns, a_live, tile):
    vmem = pl.BlockSpec(memory_space=pltpu.VMEM)
    return pl.pallas_call(
        payload_rows,
        out_shape=jax.ShapeDtypeStruct((PIECES, PIECE + META, BS), jnp.bfloat16),
        in_specs=[vmem, vmem, pl.BlockSpec(memory_space=pltpu.HBM)],
        out_specs=pl.BlockSpec(memory_space=pl.ANY),
        scratch_shapes=[
            pltpu.VMEM((META, BS), jnp.float32),
            pltpu.VMEM((PIECES, META, BS), jnp.bfloat16),
            pltpu.SemaphoreType.DMA((2,)),
        ],
        compiler_params=pltpu.CompilerParams(vmem_limit_bytes=4 * 1024 * 1024),
    )(a_columns, a_live, pltpu.with_memory_space_constraint(tile, pltpu.HBM))


def on_device(a_blocks, a_columns, a_live, owner_map, b_blocks, b_columns):
    tile = a_blocks.reshape(PIECES, PIECE, BS)
    cols = lax.axis_size(COL)
    got = lax.all_to_all(payload(a_columns[0, 0], a_live[0], tile), ("z", "y_lo"), 0, 0, tiled=True)
    holder = owner_map[0]
    source = (holder % Z) * Y_LO + holder // Z
    bc_here = b_columns[0, 0]
    bc_next = lax.ppermute(bc_here, COL, col_route(cols)).reshape(-1)
    bc_here = bc_here.reshape(-1)
    place = lax.axis_index("z").astype(jnp.int32)[None]
    got, bc_here, bc_next, place = lax.optimization_barrier((got, bc_here, bc_next, place))

    two = jnp.stack([lax.dynamic_index_in_dim(got, source[k], 0, keepdims=False) for k in range(2)])
    table = two[:, PIECE, :EACH].astype(jnp.int32).reshape(-1)
    own = lax.all_gather(two[:, :PIECE], "y_lo", axis=1, tiled=True)
    b_here = b_blocks[0, 0]
    b_ready, own, table = lax.optimization_barrier((b_here, own, table))
    b_next = lax.ppermute(b_ready, COL, col_route(cols))
    ahead = [own]
    back = [own]
    for step in range(3):
        ahead.append(lax.ppermute(ahead[-1], "z", z_route(1)))
        back.append(lax.ppermute(back[-1], "z", z_route(-1)))
    scalars = (place, table, bc_here, bc_next)
    near = (own, ahead[1], back[1], ahead[2], back[2])
    block = (NB, BS, BS)
    shape = jax.ShapeDtypeStruct((MB, BS, NB * BS), jnp.bfloat16)
    part = call(
        first_section,
        scalars,
        near + (b_here,),
        (),
        jax.ShapeDtypeStruct((2,) + block, jnp.float32),
        [pltpu.VMEM((2,) + block, jnp.float32), pltpu.SemaphoreType.DMA((2,))],
        6,
    )
    part, ahead[3], back[3] = lax.optimization_barrier((part, ahead[3], back[3]))
    f4 = lax.ppermute(ahead[3][:, : SPAN // 2], "z", z_route(1))
    b4 = lax.ppermute(back[3][:, SPAN // 2 :], "z", z_route(-1))
    window = call(
        three_rows,
        scalars,
        near + (ahead[3], back[3], b_here, b_next),
        (part,),
        shape,
        [
            pltpu.VMEM((3,) + block, jnp.float32),
            pltpu.VMEM((3, BS, NB * BS), jnp.bfloat16),
            pltpu.SemaphoreType.DMA((5,)),
        ],
        12,
    )
    window = call(
        last_row,
        scalars,
        (ahead[3], back[3], f4, b4, b_here, b_next),
        (window,),
        shape,
        [pltpu.VMEM(block, jnp.float32), pltpu.VMEM((BS, NB * BS), jnp.bfloat16), pltpu.SemaphoreType.DMA((1,))],
        6,
        alias=True,
    )
    return window[None, None]


def solution(mesh):
    fine = Mesh(mesh.devices.reshape(Y_LO, Z, 2, 4, 2), ROW + COL)
    row, col = ROW, COL
    return jax.shard_map(
        on_device,
        mesh=fine,
        in_specs=(
            P(row, col, None, None, None, None),
            P(row, col, None, None),
            P(row, col, None),
            P(col, None),
            P(row, col, None, None, None),
            P(row, col, None, None),
        ),
        out_specs=P(row, col, None, None, None),
        check_vma=False,
    )
```

```python
import jax
import jax.numpy as jnp
from jax import lax
from jax.experimental import pallas as pl
from jax.experimental.pallas import tpu as pltpu
from jax.sharding import Mesh, PartitionSpec as P

BS = 256
MB = 4
NZA = 3
KB = 4
NZB = 2
NB = 4
Y_LO = 4
Z = 8
COL = ("y_hi", "x", "core")
ROW = ("y_lo", "z")
PIECES = Y_LO * Z
PIECE = MB * NZA * BS // PIECES
SPAN = Y_LO * PIECE
META = 8


def z_route(distance):
    return [(i, (i + distance) % Z) for i in range(Z)]


def col_route(n):
    return [((i + 1) % n, i) for i in range(n)]


def within(n):
    return [(a, b) for a, b in col_route(n) if (b + 1) % (n // 2)]


def across(n):
    return [(a, b) for a, b in col_route(n) if not (b + 1) % (n // 2)]


EACH = MB * NZA + MB


def strips(parts):
    found = []
    at = 0
    for ref in parts:
        rows = ref.shape[1]
        off = 0
        while off < rows:
            slot = at // BS
            take = min(rows - off, (slot + 1) * BS - at)
            found.append((slot, at - slot * BS, ref, off, take))
            off += take
            at += take
    return found


def add_products(scalars, i, k, parts, b_ref, acc):
    table, pairs = scalars[1], scalars[2 + k]
    live = table[k * EACH + MB * NZA + i]
    for s in range(NZA):

        @pl.when(s < live)
        def _():
            q = table[k * EACH + s * MB + i]
            b = b_ref[q] if k == 0 else b_ref[0][q] + b_ref[1][q]
            for slot, row, ref, off, take in strips(parts):
                if slot == s:
                    product = jnp.dot(ref[k, off : off + take, :], b, preferred_element_type=jnp.float32)
                    for t in range(NZB):
                        j = pairs[q * NZB + t]
                        acc[j, row : row + take] += product[:, t * BS : (t + 1) * BS]


def on_parity(scalars, even, odd, sections, b_refs, acc):
    z = scalars[0][0]
    for bit, (away, parts) in enumerate((even, odd)):

        @pl.when(z % 2 == bit)
        def _():
            i = ((z + away + Z) % Z) // 2
            for k in sections:
                add_products(scalars, i, k, parts, b_refs[k], acc)

    return ((z + even[0] + (z % 2) * (odd[0] - even[0]) + Z) % Z) // 2


def write_row(o_s, acc, out, i, sem):
    for j in range(NB):
        o_s[:, j * BS : (j + 1) * BS] = acc[j].astype(jnp.bfloat16)
    copy = pltpu.make_async_copy(o_s, out.at[i], sem)
    copy.start()
    return copy


def first_section(*refs):
    scalars, (own, f1, b1, f2, b2, b_here, part, acc, sem) = refs[:4], refs[4:]
    acc[...] = jnp.zeros_like(acc)
    rows = (((0, (own, b1)), (-1, (f1, own))), ((-2, (f2, f1)), (1, (b1, b2))))
    copies = []
    for n, (even, odd) in enumerate(rows):
        on_parity(scalars, even, odd, (0,), (b_here,), acc.at[n])
        copies.append(pltpu.make_async_copy(acc.at[n], part.at[n], sem.at[n]))
        copies[-1].start()
    for c in copies:
        c.wait()


def three_rows(*refs):
    scalars = refs[:4]
    own, f1, b1, f2, b2, f3, b3, b_here, b_in, b_over, part, out, acc, o_s, sem = refs[4:]
    b_refs = (b_here, (b_in, b_over))
    loads = [pltpu.make_async_copy(part.at[n], acc.at[n], sem.at[n]) for n in range(2)]
    for c in loads:
        c.start()
    acc[2] = jnp.zeros_like(acc[2])
    i = on_parity(scalars, (2, (b2, b3)), (-3, (f3, f2)), (0, 1), b_refs, acc.at[2])
    writes = [write_row(o_s.at[2], acc.at[2], out, i, sem.at[2])]
    rows = (((0, (own, b1)), (-1, (f1, own))), ((-2, (f2, f1)), (1, (b1, b2))))
    for n, (even, odd) in enumerate(rows):
        loads[n].wait()
        i = on_parity(scalars, even, odd, (1,), b_refs, acc.at[n])
        writes.append(write_row(o_s.at[n], acc.at[n], out, i, sem.at[3 + n]))
    for c in writes:
        c.wait()


def last_row(*refs):
    scalars = refs[:4]
    f3, b3, f4, b4, b_here, b_in, b_over, before, out, acc, o_s, sem = refs[4:]
    acc[...] = jnp.zeros_like(acc)
    i = on_parity(scalars, (4, (f4, b4, f3)), (3, (b3, f4, b4)), (0, 1), (b_here, (b_in, b_over)), acc)
    write_row(o_s, acc, out, i, sem.at[0]).wait()


def call(kernel, scalars, held, left, out_shape, scratch, products, alias=False):
    hbm = pl.BlockSpec(memory_space=pl.ANY)
    vmem = pl.BlockSpec(memory_space=pltpu.VMEM)
    return pl.pallas_call(
        kernel,
        out_shape=out_shape,
        grid_spec=pltpu.PrefetchScalarGridSpec(
            num_scalar_prefetch=len(scalars),
            grid=(),
            in_specs=[vmem] * len(held) + [hbm] * len(left),
            out_specs=hbm,
            scratch_shapes=scratch,
        ),
        input_output_aliases={len(scalars) + len(held): 0} if alias else {},
        cost_estimate=pl.CostEstimate(flops=products * 4 * BS**3, bytes_accessed=1 << 20, transcendentals=0),
        compiler_params=pltpu.CompilerParams(vmem_limit_bytes=12 * 1024 * 1024),
    )(*scalars, *held, *left)


CHUNKS = 4


def payload_rows(a_columns, a_live, tile, out, columns, live, wide, rows, sem):
    step = PIECES // CHUNKS
    small = [
        pltpu.make_async_copy(a_columns, columns, sem.at[2 * CHUNKS]),
        pltpu.make_async_copy(a_live, live, sem.at[2 * CHUNKS + 1]),
    ]
    reads = []
    writes = []
    for c in range(CHUNKS):
        part = pl.ds(c * step, step)
        reads.append(pltpu.make_async_copy(tile.at[part], rows.at[part, :PIECE], sem.at[c]))
        writes.append(pltpu.make_async_copy(rows.at[part], out.at[part], sem.at[CHUNKS + c]))
    for c in small + reads:
        c.start()
    wide[...] = jnp.zeros_like(wide)
    for c in small:
        c.wait()
    for s in range(NZA):
        wide[:1, s * MB : (s + 1) * MB] = columns[s].astype(jnp.float32)
    wide[:1, MB * NZA : EACH] = live[...].astype(jnp.float32)
    for p in range(PIECES):
        rows[p, PIECE:, :] = wide[...].astype(jnp.bfloat16)
    for r, w in zip(reads, writes):
        r.wait()
        w.start()
    for w in writes:
        w.wait()


def payload(a_columns, a_live, tile):
    hbm = pl.BlockSpec(memory_space=pltpu.HBM)
    return pl.pallas_call(
        payload_rows,
        out_shape=jax.ShapeDtypeStruct((PIECES, PIECE + META, BS), jnp.bfloat16),
        in_specs=[hbm, hbm, hbm],
        out_specs=hbm,
        scratch_shapes=[
            pltpu.VMEM((NZA, 1, MB), jnp.int32),
            pltpu.VMEM((1, MB), jnp.int32),
            pltpu.VMEM((META, BS), jnp.float32),
            pltpu.VMEM((PIECES, PIECE + META, BS), jnp.bfloat16),
            pltpu.SemaphoreType.DMA((2 * CHUNKS + 2,)),
        ],
        compiler_params=pltpu.CompilerParams(vmem_limit_bytes=4 * 1024 * 1024),
    )(*(pltpu.with_memory_space_constraint(x, pltpu.HBM) for x in (a_columns, a_live, tile)))


def on_device(a_blocks, a_columns, a_live, owner_map, b_blocks, b_columns):
    tile = a_blocks.reshape(PIECES, PIECE, BS)
    cols = lax.axis_size(COL)
    got = lax.all_to_all(payload(a_columns[0].transpose(2, 0, 1), a_live[0], tile), ("z", "y_lo"), 0, 0, tiled=True)
    holder = owner_map[0]
    source = (holder % Z) * Y_LO + holder // Z
    bc_here = b_columns[0, 0]
    bc_next = lax.ppermute(bc_here, COL, col_route(cols)).reshape(-1)
    bc_here = bc_here.reshape(-1)
    place = lax.axis_index("z").astype(jnp.int32)[None]
    b_here = b_blocks[0, 0]
    b_in = lax.ppermute(b_here, COL, within(cols))
    got, bc_here, bc_next, place, b_in = lax.optimization_barrier((got, bc_here, bc_next, place, b_in))

    two = jnp.stack([lax.dynamic_index_in_dim(got, source[k], 0, keepdims=False) for k in range(2)])
    table = two[:, PIECE, :EACH].astype(jnp.int32).reshape(-1)
    own = lax.all_gather(two[:, :PIECE], "y_lo", axis=1, tiled=True)
    b_ready, own, table = lax.optimization_barrier((b_here, own, table))
    b_over = lax.ppermute(b_ready, COL, across(cols))
    ahead = [own]
    back = [own]
    for step in range(3):
        ahead.append(lax.ppermute(ahead[-1], "z", z_route(1)))
        back.append(lax.ppermute(back[-1], "z", z_route(-1)))
    scalars = (place, table, bc_here, bc_next)
    near = (own, ahead[1], back[1], ahead[2], back[2])
    block = (NB, BS, BS)
    shape = jax.ShapeDtypeStruct((MB, BS, NB * BS), jnp.bfloat16)
    part = call(
        first_section,
        scalars,
        near + (b_here,),
        (),
        jax.ShapeDtypeStruct((2,) + block, jnp.float32),
        [pltpu.VMEM((2,) + block, jnp.float32), pltpu.SemaphoreType.DMA((2,))],
        6,
    )
    part, ahead[3], back[3] = lax.optimization_barrier((part, ahead[3], back[3]))
    f4 = lax.ppermute(ahead[3][:, : SPAN // 2], "z", z_route(1))
    b4 = lax.ppermute(back[3][:, SPAN // 2 :], "z", z_route(-1))
    window = call(
        three_rows,
        scalars,
        near + (ahead[3], back[3], b_here, b_in, b_over),
        (part,),
        shape,
        [
            pltpu.VMEM((3,) + block, jnp.float32),
            pltpu.VMEM((3, BS, NB * BS), jnp.bfloat16),
            pltpu.SemaphoreType.DMA((5,)),
        ],
        12,
    )
    window = call(
        last_row,
        scalars,
        (ahead[3], back[3], f4, b4, b_here, b_in, b_over),
        (window,),
        shape,
        [pltpu.VMEM(block, jnp.float32), pltpu.VMEM((BS, NB * BS), jnp.bfloat16), pltpu.SemaphoreType.DMA((1,))],
        6,
        alias=True,
    )
    return window[None, None]


def solution(mesh):
    fine = Mesh(mesh.devices.reshape(Y_LO, Z, 2, 4, 2), ROW + COL)
    row, col = ROW, COL
    return jax.shard_map(
        on_device,
        mesh=fine,
        in_specs=(
            P(row, col, None, None, None, None),
            P(row, col, None, None),
            P(row, col, None),
            P(col, None),
            P(row, col, None, None, None),
            P(row, col, None, None),
        ),
        out_specs=P(row, col, None, None, None),
        check_vma=False,
    )
```

```python
import jax
import jax.numpy as jnp
from jax import lax
from jax.experimental import pallas as pl
from jax.experimental.pallas import tpu as pltpu
from jax.sharding import Mesh, PartitionSpec as P

BS = 256
MB = 4
NZA = 3
KB = 4
NZB = 2
NB = 4
Y_LO = 4
Z = 8
COL = ("y_hi", "x", "core")
ROW = ("y_lo", "z")
PIECES = Y_LO * Z
PIECE = MB * NZA * BS // PIECES
SPAN = Y_LO * PIECE
META = 8


def swap_route(toward):
    pairs = []
    for z in range(Z):
        for core in range(2):
            side = toward if (z + core) % 2 == 0 else -toward
            pairs.append((z * 2 + core, ((z + side) % Z) * 2 + core))
    return pairs


def swapped(value, toward):
    return lax.ppermute(value, ("z", "core"), swap_route(toward))


def col_route(n):
    return [((i + 1) % n, i) for i in range(n)]


def within(n):
    return [(a, b) for a, b in col_route(n) if (b + 1) % (n // 2)]


def across(n):
    return [(a, b) for a, b in col_route(n) if not (b + 1) % (n // 2)]


EACH = MB * NZA + MB


def strips(parts):
    found = []
    at = 0
    for ref, base in parts:
        off = 0
        while off < SPAN:
            slot = at // BS
            take = min(SPAN - off, (slot + 1) * BS - at)
            found.append((slot, at - slot * BS, ref, base + off, take))
            off += take
            at += take
    return found


def add_products(scalars, i, k, parts, b_ref, acc):
    table, pairs = scalars[1], scalars[2 + k]
    live = table[k * EACH + MB * NZA + i]
    for s in range(NZA):

        @pl.when(s < live)
        def _():
            q = table[k * EACH + s * MB + i]
            b = b_ref[q] if k == 0 else b_ref[0][q] + b_ref[1][q]
            for slot, row, ref, off, take in strips(parts):
                if slot == s:
                    product = jnp.dot(ref[k, off : off + take, :], b, preferred_element_type=jnp.float32)
                    for t in range(NZB):
                        j = pairs[q * NZB + t]
                        acc[j, row : row + take] += product[:, t * BS : (t + 1) * BS]


def on_parity(scalars, even, odd, sections, b_refs, acc):
    z = scalars[0][0]
    for bit, (away, parts) in enumerate((even, odd)):

        @pl.when(z % 2 == bit)
        def _():
            i = ((z + away + Z) % Z) // 2
            for k in sections:
                add_products(scalars, i, k, parts, b_refs[k], acc)

    return ((z + even[0] + (z % 2) * (odd[0] - even[0]) + Z) % Z) // 2


def write_row(o_s, acc, out, i, sem):
    for j in range(NB):
        o_s[:, j * BS : (j + 1) * BS] = acc[j].astype(jnp.bfloat16)
    copy = pltpu.make_async_copy(o_s, out.at[i], sem)
    copy.start()
    return copy


def near_rows(own, r1, r2):
    here = ((0, ((own, 0), (r1, 0))), (-1, ((r1, 0), (own, 0))))
    next_to = ((-2, ((r2, SPAN), (r2, 0))), (1, ((r2, 0), (r2, SPAN))))
    return here, next_to


def first_section(*refs):
    scalars, (own, r1, r2, b_here, part, acc, sem) = refs[:4], refs[4:]
    acc[...] = jnp.zeros_like(acc)
    copies = []
    for n, (even, odd) in enumerate(near_rows(own, r1, r2)):
        on_parity(scalars, even, odd, (0,), (b_here,), acc.at[n])
        copies.append(pltpu.make_async_copy(acc.at[n], part.at[n], sem.at[n]))
        copies[-1].start()
    for c in copies:
        c.wait()


def three_rows(*refs):
    scalars = refs[:4]
    own, r1, r2, r3, b_here, b_in, b_over, part, out, acc, o_s, sem = refs[4:]
    b_refs = (b_here, (b_in, b_over))
    loads = [pltpu.make_async_copy(part.at[n], acc.at[n], sem.at[n]) for n in range(2)]
    for c in loads:
        c.start()
    acc[2] = jnp.zeros_like(acc[2])
    even, odd = (2, ((r3, 0), (r3, SPAN))), (-3, ((r3, SPAN), (r3, 0)))
    i = on_parity(scalars, even, odd, (0, 1), b_refs, acc.at[2])
    writes = [write_row(o_s.at[2], acc.at[2], out, i, sem.at[2])]
    for n, (even, odd) in enumerate(near_rows(own, r1, r2)):
        loads[n].wait()
        i = on_parity(scalars, even, odd, (1,), b_refs, acc.at[n])
        writes.append(write_row(o_s.at[n], acc.at[n], out, i, sem.at[3 + n]))
    for c in writes:
        c.wait()


def last_row(*refs):
    scalars = refs[:4]
    r4, b_here, b_in, b_over, before, out, acc, o_s, sem = refs[4:]
    acc[...] = jnp.zeros_like(acc)
    even, odd = (-4, ((r4, SPAN), (r4, 0))), (3, ((r4, 0), (r4, SPAN)))
    i = on_parity(scalars, even, odd, (0, 1), (b_here, (b_in, b_over)), acc)
    write_row(o_s, acc, out, i, sem.at[0]).wait()


def call(kernel, scalars, held, left, out_shape, scratch, products, alias=False):
    hbm = pl.BlockSpec(memory_space=pl.ANY)
    vmem = pl.BlockSpec(memory_space=pltpu.VMEM)
    return pl.pallas_call(
        kernel,
        out_shape=out_shape,
        grid_spec=pltpu.PrefetchScalarGridSpec(
            num_scalar_prefetch=len(scalars),
            grid=(),
            in_specs=[vmem] * len(held) + [hbm] * len(left),
            out_specs=hbm,
            scratch_shapes=scratch,
        ),
        input_output_aliases={len(scalars) + len(held): 0} if alias else {},
        cost_estimate=pl.CostEstimate(flops=products * 4 * BS**3, bytes_accessed=1 << 20, transcendentals=0),
        compiler_params=pltpu.CompilerParams(vmem_limit_bytes=12 * 1024 * 1024),
    )(*scalars, *held, *left)


def payload_rows(shift, a_columns, a_live, tile, out, columns, live, wide, rows, sem):
    small = [
        pltpu.make_async_copy(a_columns, columns, sem.at[2 * Z]),
        pltpu.make_async_copy(a_live, live, sem.at[2 * Z + 1]),
    ]
    reads = []
    writes = []
    for c in range(Z):
        part = pl.ds(c * Y_LO, Y_LO)
        first = ((c + Z - shift[0]) % Z) * Y_LO
        reads.append(pltpu.make_async_copy(tile.at[pl.ds(first, Y_LO)], rows.at[part, :PIECE], sem.at[c]))
        writes.append(pltpu.make_async_copy(rows.at[part], out.at[part], sem.at[Z + c]))
    for c in small + reads:
        c.start()
    wide[...] = jnp.zeros_like(wide)
    for c in small:
        c.wait()
    for s in range(NZA):
        wide[:1, s * MB : (s + 1) * MB] = columns[s].astype(jnp.float32)
    wide[:1, MB * NZA : EACH] = live[...].astype(jnp.float32)
    for p in range(PIECES):
        rows[p, PIECE:, :] = wide[...].astype(jnp.bfloat16)
    for r, w in zip(reads, writes):
        r.wait()
        w.start()
    for w in writes:
        w.wait()


def payload(core, a_columns, a_live, tile):
    hbm = pl.BlockSpec(memory_space=pltpu.HBM)
    return pl.pallas_call(
        payload_rows,
        out_shape=jax.ShapeDtypeStruct((PIECES, PIECE + META, BS), jnp.bfloat16),
        grid_spec=pltpu.PrefetchScalarGridSpec(
            num_scalar_prefetch=1,
            grid=(),
            in_specs=[hbm, hbm, hbm],
            out_specs=hbm,
            scratch_shapes=[
                pltpu.VMEM((NZA, 1, MB), jnp.int32),
                pltpu.VMEM((1, MB), jnp.int32),
                pltpu.VMEM((META, BS), jnp.float32),
                pltpu.VMEM((PIECES, PIECE + META, BS), jnp.bfloat16),
                pltpu.SemaphoreType.DMA((2 * Z + 2,)),
            ],
        ),
        compiler_params=pltpu.CompilerParams(vmem_limit_bytes=4 * 1024 * 1024),
    )(core[None], *(pltpu.with_memory_space_constraint(x, pltpu.HBM) for x in (a_columns, a_live, tile)))


def on_device(a_blocks, a_columns, a_live, owner_map, b_blocks, b_columns):
    tile = a_blocks.reshape(PIECES, PIECE, BS)
    cols = lax.axis_size(COL)
    core = lax.axis_index("core").astype(jnp.int32)
    sent = payload(core, a_columns[0].transpose(2, 0, 1), a_live[0], tile)
    got = lax.all_to_all(sent, ("z", "y_lo"), 0, 0, tiled=True)
    holder = owner_map[0]
    source = (holder % Z) * Y_LO + holder // Z
    bc_here = b_columns[0, 0]
    bc_next = lax.ppermute(bc_here, COL, col_route(cols)).reshape(-1)
    bc_here = bc_here.reshape(-1)
    place = ((lax.axis_index("z").astype(jnp.int32) + Z - core) % Z)[None]
    b_here = b_blocks[0, 0]
    b_in = lax.ppermute(b_here, COL, within(cols))
    got, bc_here, bc_next, place, b_in = lax.optimization_barrier((got, bc_here, bc_next, place, b_in))

    two = jnp.stack([lax.dynamic_index_in_dim(got, source[k], 0, keepdims=False) for k in range(2)])
    table = two[:, PIECE, :EACH].astype(jnp.int32).reshape(-1)
    own = lax.all_gather(two[:, :PIECE], "y_lo", axis=1, tiled=True)
    b_ready, own, table = lax.optimization_barrier((b_here, own, table))
    b_over = lax.ppermute(b_ready, COL, across(cols))
    r1 = swapped(own, 1)
    r2 = swapped(jnp.concatenate([own, r1], axis=1), -1)
    r3 = swapped(r2, 1)
    scalars = (place, table, bc_here, bc_next)
    near = (own, r1, r2)
    block = (NB, BS, BS)
    shape = jax.ShapeDtypeStruct((MB, BS, NB * BS), jnp.bfloat16)
    part = call(
        first_section,
        scalars,
        near + (b_here,),
        (),
        jax.ShapeDtypeStruct((2,) + block, jnp.float32),
        [pltpu.VMEM((2,) + block, jnp.float32), pltpu.SemaphoreType.DMA((2,))],
        6,
    )
    part, r3, b_over = lax.optimization_barrier((part, r3, b_over))
    r4 = swapped(r3, -1)
    window = call(
        three_rows,
        scalars,
        near + (r3, b_here, b_in, b_over),
        (part,),
        shape,
        [
            pltpu.VMEM((3,) + block, jnp.float32),
            pltpu.VMEM((3, BS, NB * BS), jnp.bfloat16),
            pltpu.SemaphoreType.DMA((5,)),
        ],
        12,
    )
    window = call(
        last_row,
        scalars,
        (r4, b_here, b_in, b_over),
        (window,),
        shape,
        [pltpu.VMEM(block, jnp.float32), pltpu.VMEM((BS, NB * BS), jnp.bfloat16), pltpu.SemaphoreType.DMA((1,))],
        6,
        alias=True,
    )
    return window[None, None]


def solution(mesh):
    fine = Mesh(mesh.devices.reshape(Y_LO, Z, 2, 4, 2), ROW + COL)
    row, col = ROW, COL
    return jax.shard_map(
        on_device,
        mesh=fine,
        in_specs=(
            P(row, col, None, None, None, None),
            P(row, col, None, None),
            P(row, col, None),
            P(col, None),
            P(row, col, None, None, None),
            P(row, col, None, None),
        ),
        out_specs=P(row, col, None, None, None),
        check_vma=False,
    )
```

```python
import jax
import jax.numpy as jnp
from jax import lax
from jax.experimental import pallas as pl
from jax.experimental.pallas import tpu as pltpu
from jax.sharding import Mesh, PartitionSpec as P

BS = 256
MB = 4
NZA = 3
KB = 4
NZB = 2
NB = 4
Y_LO = 4
Z = 8
COL = ("y_hi", "x", "core")
ROW = ("y_lo", "z")
PIECES = Y_LO * Z
PIECE = MB * NZA * BS // PIECES
SPAN = Y_LO * PIECE
META = 8


def z_route(distance):
    return [(i, (i + distance) % Z) for i in range(Z)]


def col_route(n):
    return [((i + 1) % n, i) for i in range(n)]


def within(n):
    return [(a, b) for a, b in col_route(n) if (b + 1) % (n // 2)]


def across(n):
    return [(a, b) for a, b in col_route(n) if not (b + 1) % (n // 2)]


EACH = MB * NZA + MB


def strips(parts):
    found = []
    at = 0
    for ref in parts:
        rows = ref.shape[1]
        off = 0
        while off < rows:
            slot = at // BS
            take = min(rows - off, (slot + 1) * BS - at)
            found.append((slot, at - slot * BS, ref, off, take))
            off += take
            at += take
    return found


def add_products(scalars, i, k, parts, b_ref, acc):
    table, pairs = scalars[1], scalars[2 + k]
    live = table[k * EACH + MB * NZA + i]
    for s in range(NZA):

        @pl.when(s < live)
        def _():
            q = table[k * EACH + s * MB + i]
            b = b_ref[q] if k == 0 else b_ref[0][q] + b_ref[1][q]
            for slot, row, ref, off, take in strips(parts):
                if slot == s:
                    product = jnp.dot(ref[k, off : off + take, :], b, preferred_element_type=jnp.float32)
                    for t in range(NZB):
                        j = pairs[q * NZB + t]
                        acc[j, row : row + take] += product[:, t * BS : (t + 1) * BS]


def on_parity(scalars, even, odd, sections, b_refs, acc):
    z = scalars[0][0]
    for bit, (away, parts) in enumerate((even, odd)):

        @pl.when(z % 2 == bit)
        def _():
            i = ((z + away + Z) % Z) // 2
            for k in sections:
                add_products(scalars, i, k, parts, b_refs[k], acc)

    return ((z + even[0] + (z % 2) * (odd[0] - even[0]) + Z) % Z) // 2


def write_row(o_s, acc, out, i, sem):
    for j in range(NB):
        o_s[:, j * BS : (j + 1) * BS] = acc[j].astype(jnp.bfloat16)
    copy = pltpu.make_async_copy(o_s, out.at[i], sem)
    copy.start()
    return copy


def three_rows(*refs):
    scalars = refs[:4]
    own, f1, b1, f2, b2, f3, b3, b_here, b_in, b_over, out, acc, o_s, sem = refs[4:]
    b_refs = (b_here, (b_in, b_over))
    rows = (
        ((0, (own, b1)), (-1, (f1, own))),
        ((-2, (f2, f1)), (1, (b1, b2))),
        ((2, (b2, b3)), (-3, (f3, f2))),
    )
    acc[...] = jnp.zeros_like(acc)
    writes = []
    for n, (even, odd) in enumerate(rows):
        i = on_parity(scalars, even, odd, (0, 1), b_refs, acc.at[n])
        writes.append(write_row(o_s.at[n], acc.at[n], out, i, sem.at[n]))
    for c in writes:
        c.wait()


def last_row(*refs):
    scalars = refs[:4]
    f3, b3, f4, b4, b_here, b_in, b_over, before, out, acc, o_s, sem = refs[4:]
    acc[...] = jnp.zeros_like(acc)
    i = on_parity(scalars, (4, (f4, b4, f3)), (3, (b3, f4, b4)), (0, 1), (b_here, (b_in, b_over)), acc)
    write_row(o_s, acc, out, i, sem.at[0]).wait()


def call(kernel, scalars, held, left, out_shape, scratch, products, alias=False):
    hbm = pl.BlockSpec(memory_space=pl.ANY)
    vmem = pl.BlockSpec(memory_space=pltpu.VMEM)
    return pl.pallas_call(
        kernel,
        out_shape=out_shape,
        grid_spec=pltpu.PrefetchScalarGridSpec(
            num_scalar_prefetch=len(scalars),
            grid=(),
            in_specs=[vmem] * len(held) + [hbm] * len(left),
            out_specs=hbm,
            scratch_shapes=scratch,
        ),
        input_output_aliases={len(scalars) + len(held): 0} if alias else {},
        cost_estimate=pl.CostEstimate(flops=products * 4 * BS**3, bytes_accessed=1 << 20, transcendentals=0),
        compiler_params=pltpu.CompilerParams(vmem_limit_bytes=12 * 1024 * 1024),
    )(*scalars, *held, *left)


CHUNKS = 4


def payload_rows(a_columns, a_live, tile, out, columns, live, wide, rows, sem):
    step = PIECES // CHUNKS
    small = [
        pltpu.make_async_copy(a_columns, columns, sem.at[2 * CHUNKS]),
        pltpu.make_async_copy(a_live, live, sem.at[2 * CHUNKS + 1]),
    ]
    reads = []
    writes = []
    for c in range(CHUNKS):
        part = pl.ds(c * step, step)
        reads.append(pltpu.make_async_copy(tile.at[part], rows.at[part, :PIECE], sem.at[c]))
        writes.append(pltpu.make_async_copy(rows.at[part], out.at[part], sem.at[CHUNKS + c]))
    for c in small + reads:
        c.start()
    wide[...] = jnp.zeros_like(wide)
    for c in small:
        c.wait()
    for s in range(NZA):
        wide[:1, s * MB : (s + 1) * MB] = columns[s].astype(jnp.float32)
    wide[:1, MB * NZA : EACH] = live[...].astype(jnp.float32)
    for p in range(PIECES):
        rows[p, PIECE:, :] = wide[...].astype(jnp.bfloat16)
    for r, w in zip(reads, writes):
        r.wait()
        w.start()
    for w in writes:
        w.wait()


def payload(a_columns, a_live, tile):
    hbm = pl.BlockSpec(memory_space=pltpu.HBM)
    return pl.pallas_call(
        payload_rows,
        out_shape=jax.ShapeDtypeStruct((PIECES, PIECE + META, BS), jnp.bfloat16),
        in_specs=[hbm, hbm, hbm],
        out_specs=hbm,
        scratch_shapes=[
            pltpu.VMEM((NZA, 1, MB), jnp.int32),
            pltpu.VMEM((1, MB), jnp.int32),
            pltpu.VMEM((META, BS), jnp.float32),
            pltpu.VMEM((PIECES, PIECE + META, BS), jnp.bfloat16),
            pltpu.SemaphoreType.DMA((2 * CHUNKS + 2,)),
        ],
        compiler_params=pltpu.CompilerParams(vmem_limit_bytes=4 * 1024 * 1024),
    )(*(pltpu.with_memory_space_constraint(x, pltpu.HBM) for x in (a_columns, a_live, tile)))


def on_device(a_blocks, a_columns, a_live, owner_map, b_blocks, b_columns):
    tile = a_blocks.reshape(PIECES, PIECE, BS)
    cols = lax.axis_size(COL)
    got = lax.all_to_all(payload(a_columns[0].transpose(2, 0, 1), a_live[0], tile), ("z", "y_lo"), 0, 0, tiled=True)
    holder = owner_map[0]
    source = (holder % Z) * Y_LO + holder // Z
    bc_here = b_columns[0, 0]
    bc_next = lax.ppermute(bc_here, COL, col_route(cols)).reshape(-1)
    bc_here = bc_here.reshape(-1)
    place = lax.axis_index("z").astype(jnp.int32)[None]
    b_here = b_blocks[0, 0]
    b_in = lax.ppermute(b_here, COL, within(cols))
    got, bc_here, bc_next, place, b_in = lax.optimization_barrier((got, bc_here, bc_next, place, b_in))

    two = jnp.stack([lax.dynamic_index_in_dim(got, source[k], 0, keepdims=False) for k in range(2)])
    table = two[:, PIECE, :EACH].astype(jnp.int32).reshape(-1)
    own = lax.all_gather(two[:, :PIECE], "y_lo", axis=1, tiled=True)
    b_ready, own, table = lax.optimization_barrier((b_here, own, table))
    b_over = lax.ppermute(b_ready, COL, across(cols))
    ahead = [own]
    back = [own]
    for step in range(3):
        ahead.append(lax.ppermute(ahead[-1], "z", z_route(1)))
        back.append(lax.ppermute(back[-1], "z", z_route(-1)))
    scalars = (place, table, bc_here, bc_next)
    near = (own, ahead[1], back[1], ahead[2], back[2])
    block = (NB, BS, BS)
    shape = jax.ShapeDtypeStruct((MB, BS, NB * BS), jnp.bfloat16)
    f4 = lax.ppermute(ahead[2][:, : SPAN // 2], "z", z_route(2))
    b4 = lax.ppermute(back[2][:, SPAN // 2 :], "z", z_route(-2))
    window = call(
        three_rows,
        scalars,
        near + (ahead[3], back[3], b_here, b_in, b_over),
        (),
        shape,
        [
            pltpu.VMEM((3,) + block, jnp.float32),
            pltpu.VMEM((3, BS, NB * BS), jnp.bfloat16),
            pltpu.SemaphoreType.DMA((3,)),
        ],
        18,
    )
    window = call(
        last_row,
        scalars,
        (ahead[3], back[3], f4, b4, b_here, b_in, b_over),
        (window,),
        shape,
        [pltpu.VMEM(block, jnp.float32), pltpu.VMEM((BS, NB * BS), jnp.bfloat16), pltpu.SemaphoreType.DMA((1,))],
        6,
        alias=True,
    )
    return window[None, None]


def solution(mesh):
    fine = Mesh(mesh.devices.reshape(Y_LO, Z, 2, 4, 2), ROW + COL)
    row, col = ROW, COL
    return jax.shard_map(
        on_device,
        mesh=fine,
        in_specs=(
            P(row, col, None, None, None, None),
            P(row, col, None, None),
            P(row, col, None),
            P(col, None),
            P(row, col, None, None, None),
            P(row, col, None, None),
        ),
        out_specs=P(row, col, None, None, None),
        check_vma=False,
    )
```

```python
import jax
import jax.numpy as jnp
from jax import lax
from jax.experimental import pallas as pl
from jax.experimental.pallas import tpu as pltpu
from jax.sharding import Mesh, PartitionSpec as P

BS = 256
MB = 4
NZA = 3
KB = 4
NZB = 2
NB = 4
Y_LO = 4
Z = 8
COL = ("y_hi", "x", "core")
ROW = ("y_lo", "z")
PIECES = Y_LO * Z
PIECE = MB * NZA * BS // PIECES
SPAN = Y_LO * PIECE
META = 8


def z_route(distance):
    return [(i, (i + distance) % Z) for i in range(Z)]


def col_route(n):
    return [((i + 1) % n, i) for i in range(n)]


def within(n):
    return [(a, b) for a, b in col_route(n) if (b + 1) % (n // 2)]


def across(n):
    return [(a, b) for a, b in col_route(n) if not (b + 1) % (n // 2)]


EACH = MB * NZA + MB


def strips(parts):
    found = []
    at = 0
    for ref in parts:
        rows = ref.shape[1]
        off = 0
        while off < rows:
            slot = at // BS
            take = min(rows - off, (slot + 1) * BS - at)
            found.append((slot, at - slot * BS, ref, off, take))
            off += take
            at += take
    return found


def add_products(scalars, i, k, parts, b_ref, acc):
    table, pairs = scalars[1], scalars[2 + k]
    live = table[k * EACH + MB * NZA + i]
    for s in range(NZA):

        @pl.when(s < live)
        def _():
            q = table[k * EACH + s * MB + i]
            b = b_ref[q] if k == 0 else b_ref[0][q] + b_ref[1][q]
            for slot, row, ref, off, take in strips(parts):
                if slot == s:
                    product = jnp.dot(ref[k, off : off + take, :], b, preferred_element_type=jnp.float32)
                    for t in range(NZB):
                        j = pairs[q * NZB + t]
                        acc[j, row : row + take] += product[:, t * BS : (t + 1) * BS]


def on_parity(scalars, even, odd, sections, b_refs, acc):
    z = scalars[0][0]
    for bit, (away, parts) in enumerate((even, odd)):

        @pl.when(z % 2 == bit)
        def _():
            i = ((z + away + Z) % Z) // 2
            for k in sections:
                add_products(scalars, i, k, parts, b_refs[k], acc)

    return ((z + even[0] + (z % 2) * (odd[0] - even[0]) + Z) % Z) // 2


def write_row(o_s, acc, out, i, sem):
    for j in range(NB):
        o_s[:, j * BS : (j + 1) * BS] = acc[j].astype(jnp.bfloat16)
    copy = pltpu.make_async_copy(o_s, out.at[i], sem)
    copy.start()
    return copy


def two_rows(*refs):
    scalars = refs[:4]
    own, f1, b1, f2, b2, b_here, b_in, b_over, out, acc, o_s, sem = refs[4:]
    rows = (((0, (own, b1)), (-1, (f1, own))), ((-2, (f2, f1)), (1, (b1, b2))))
    acc[...] = jnp.zeros_like(acc)
    writes = []
    for n, (even, odd) in enumerate(rows):
        i = on_parity(scalars, even, odd, (0, 1), (b_here, (b_in, b_over)), acc.at[n])
        writes.append(write_row(o_s.at[n], acc.at[n], out, i, sem.at[n]))
    for c in writes:
        c.wait()


def third_row(*refs):
    scalars = refs[:4]
    f2, b2, f3, b3, b_here, b_in, b_over, before, out, acc, o_s, sem = refs[4:]
    acc[...] = jnp.zeros_like(acc)
    i = on_parity(scalars, (2, (b2, b3)), (-3, (f3, f2)), (0, 1), (b_here, (b_in, b_over)), acc)
    write_row(o_s, acc, out, i, sem.at[0]).wait()


def last_row(*refs):
    scalars = refs[:4]
    f3, b3, f4, b4, b_here, b_in, b_over, before, out, acc, o_s, sem = refs[4:]
    acc[...] = jnp.zeros_like(acc)
    i = on_parity(scalars, (4, (f4, b4, f3)), (3, (b3, f4, b4)), (0, 1), (b_here, (b_in, b_over)), acc)
    write_row(o_s, acc, out, i, sem.at[0]).wait()


def call(kernel, scalars, held, left, out_shape, scratch, products, alias=False):
    hbm = pl.BlockSpec(memory_space=pl.ANY)
    vmem = pl.BlockSpec(memory_space=pltpu.VMEM)
    return pl.pallas_call(
        kernel,
        out_shape=out_shape,
        grid_spec=pltpu.PrefetchScalarGridSpec(
            num_scalar_prefetch=len(scalars),
            grid=(),
            in_specs=[vmem] * len(held) + [hbm] * len(left),
            out_specs=hbm,
            scratch_shapes=scratch,
        ),
        input_output_aliases={len(scalars) + len(held): 0} if alias else {},
        cost_estimate=pl.CostEstimate(flops=products * 4 * BS**3, bytes_accessed=1 << 20, transcendentals=0),
        compiler_params=pltpu.CompilerParams(vmem_limit_bytes=12 * 1024 * 1024),
    )(*scalars, *held, *left)


CHUNKS = 4


def payload_rows(a_columns, a_live, tile, out, columns, live, wide, rows, sem):
    step = PIECES // CHUNKS
    small = [
        pltpu.make_async_copy(a_columns, columns, sem.at[2 * CHUNKS]),
        pltpu.make_async_copy(a_live, live, sem.at[2 * CHUNKS + 1]),
    ]
    reads = []
    writes = []
    for c in range(CHUNKS):
        part = pl.ds(c * step, step)
        reads.append(pltpu.make_async_copy(tile.at[part], rows.at[part, :PIECE], sem.at[c]))
        writes.append(pltpu.make_async_copy(rows.at[part], out.at[part], sem.at[CHUNKS + c]))
    for c in small + reads:
        c.start()
    wide[...] = jnp.zeros_like(wide)
    for c in small:
        c.wait()
    for s in range(NZA):
        wide[:1, s * MB : (s + 1) * MB] = columns[s].astype(jnp.float32)
    wide[:1, MB * NZA : EACH] = live[...].astype(jnp.float32)
    for p in range(PIECES):
        rows[p, PIECE:, :] = wide[...].astype(jnp.bfloat16)
    for r, w in zip(reads, writes):
        r.wait()
        w.start()
    for w in writes:
        w.wait()


def payload(a_columns, a_live, tile):
    hbm = pl.BlockSpec(memory_space=pltpu.HBM)
    return pl.pallas_call(
        payload_rows,
        out_shape=jax.ShapeDtypeStruct((PIECES, PIECE + META, BS), jnp.bfloat16),
        in_specs=[hbm, hbm, hbm],
        out_specs=hbm,
        scratch_shapes=[
            pltpu.VMEM((NZA, 1, MB), jnp.int32),
            pltpu.VMEM((1, MB), jnp.int32),
            pltpu.VMEM((META, BS), jnp.float32),
            pltpu.VMEM((PIECES, PIECE + META, BS), jnp.bfloat16),
            pltpu.SemaphoreType.DMA((2 * CHUNKS + 2,)),
        ],
        compiler_params=pltpu.CompilerParams(vmem_limit_bytes=4 * 1024 * 1024),
    )(*(pltpu.with_memory_space_constraint(x, pltpu.HBM) for x in (a_columns, a_live, tile)))


def on_device(a_blocks, a_columns, a_live, owner_map, b_blocks, b_columns):
    tile = a_blocks.reshape(PIECES, PIECE, BS)
    cols = lax.axis_size(COL)
    got = lax.all_to_all(payload(a_columns[0].transpose(2, 0, 1), a_live[0], tile), ("z", "y_lo"), 0, 0, tiled=True)
    holder = owner_map[0]
    source = (holder % Z) * Y_LO + holder // Z
    bc_here = b_columns[0, 0]
    bc_next = lax.ppermute(bc_here, COL, col_route(cols)).reshape(-1)
    bc_here = bc_here.reshape(-1)
    place = lax.axis_index("z").astype(jnp.int32)[None]
    b_here = b_blocks[0, 0]
    b_in = lax.ppermute(b_here, COL, within(cols))
    got, bc_here, bc_next, place, b_in = lax.optimization_barrier((got, bc_here, bc_next, place, b_in))

    two = jnp.stack([lax.dynamic_index_in_dim(got, source[k], 0, keepdims=False) for k in range(2)])
    table = two[:, PIECE, :EACH].astype(jnp.int32).reshape(-1)
    own = lax.all_gather(two[:, :PIECE], "y_lo", axis=1, tiled=True)
    b_ready, own, table = lax.optimization_barrier((b_here, own, table))
    b_over = lax.ppermute(b_ready, COL, across(cols))
    ahead = [own]
    back = [own]
    for step in range(3):
        ahead.append(lax.ppermute(ahead[-1], "z", z_route(1)))
        back.append(lax.ppermute(back[-1], "z", z_route(-1)))
    scalars = (place, table, bc_here, bc_next)
    near = (own, ahead[1], back[1], ahead[2], back[2])
    block = (NB, BS, BS)
    shape = jax.ShapeDtypeStruct((MB, BS, NB * BS), jnp.bfloat16)
    f4 = lax.ppermute(ahead[2][:, : SPAN // 2], "z", z_route(2))
    b4 = lax.ppermute(back[2][:, SPAN // 2 :], "z", z_route(-2))
    b_all = (b_here, b_in, b_over)
    wide = [pltpu.VMEM((2,) + block, jnp.float32), pltpu.VMEM((2, BS, NB * BS), jnp.bfloat16), pltpu.SemaphoreType.DMA((2,))]
    slim = [pltpu.VMEM(block, jnp.float32), pltpu.VMEM((BS, NB * BS), jnp.bfloat16), pltpu.SemaphoreType.DMA((1,))]
    window = call(two_rows, scalars, near + b_all, (), shape, wide, 12)
    window = call(third_row, scalars, near[3:] + (ahead[3], back[3]) + b_all, (window,), shape, slim, 6, alias=True)
    window = call(last_row, scalars, (ahead[3], back[3], f4, b4) + b_all, (window,), shape, slim, 6, alias=True)
    return window[None, None]


def solution(mesh):
    fine = Mesh(mesh.devices.reshape(Y_LO, Z, 2, 4, 2), ROW + COL)
    row, col = ROW, COL
    return jax.shard_map(
        on_device,
        mesh=fine,
        in_specs=(
            P(row, col, None, None, None, None),
            P(row, col, None, None),
            P(row, col, None),
            P(col, None),
            P(row, col, None, None, None),
            P(row, col, None, None),
        ),
        out_specs=P(row, col, None, None, None),
        check_vma=False,
    )
```

```python
import jax
import jax.numpy as jnp
from jax import lax
from jax.experimental import pallas as pl
from jax.experimental.pallas import tpu as pltpu
from jax.sharding import Mesh, PartitionSpec as P

BS = 256
MB = 4
NZA = 3
KB = 4
NZB = 2
NB = 4
Y_LO = 4
Z = 8
COL = ("y_hi", "x", "core")
ROW = ("y_lo", "z")
PIECES = Y_LO * Z
PIECE = MB * NZA * BS // PIECES
SPAN = Y_LO * PIECE
META = 8


def z_route(distance):
    return [(i, (i + distance) % Z) for i in range(Z)]


def col_route(n):
    return [((i + 1) % n, i) for i in range(n)]


def within(n):
    return [(a, b) for a, b in col_route(n) if (b + 1) % (n // 2)]


def across(n):
    return [(a, b) for a, b in col_route(n) if not (b + 1) % (n // 2)]


EACH = MB * NZA + MB


def strips(parts):
    found = []
    at = 0
    for ref in parts:
        rows = ref.shape[1]
        off = 0
        while off < rows:
            slot = at // BS
            take = min(rows - off, (slot + 1) * BS - at)
            found.append((slot, at - slot * BS, ref, off, take))
            off += take
            at += take
    return found


def add_products(scalars, i, k, parts, b_ref, acc):
    table, pairs = scalars[1], scalars[2 + k]
    live = table[k * EACH + MB * NZA + i]
    for s in range(NZA):

        @pl.when(s < live)
        def _():
            q = table[k * EACH + s * MB + i]
            b = b_ref[q] if k == 0 else b_ref[0][q] + b_ref[1][q]
            for slot, row, ref, off, take in strips(parts):
                if slot == s:
                    product = jnp.dot(ref[k, off : off + take, :], b, preferred_element_type=jnp.float32)
                    for t in range(NZB):
                        j = pairs[q * NZB + t]
                        acc[j, row : row + take] += product[:, t * BS : (t + 1) * BS]


def on_parity(scalars, even, odd, sections, b_refs, acc):
    z = scalars[0][0]
    for bit, (away, parts) in enumerate((even, odd)):

        @pl.when(z % 2 == bit)
        def _():
            i = ((z + away + Z) % Z) // 2
            for k in sections:
                add_products(scalars, i, k, parts, b_refs[k], acc)

    return ((z + even[0] + (z % 2) * (odd[0] - even[0]) + Z) % Z) // 2


def write_row(o_s, acc, out, i, sem):
    for j in range(NB):
        o_s[:, j * BS : (j + 1) * BS] = acc[j].astype(jnp.bfloat16)
    copy = pltpu.make_async_copy(o_s, out.at[i], sem)
    copy.start()
    return copy


def two_rows(*refs):
    scalars = refs[:4]
    own, b1, f1, b2, f2, b_here, b_in, b_over, out, acc, o_s, sem = refs[4:]
    rows = (((0, (own, b1)), (-1, (f1, own))), ((-2, (f2, f1)), (1, (b1, b2))))
    acc[...] = jnp.zeros_like(acc)
    writes = []
    for n, (even, odd) in enumerate(rows):
        i = on_parity(scalars, even, odd, (0, 1), (b_here, (b_in, b_over)), acc.at[n])
        writes.append(write_row(o_s.at[n], acc.at[n], out, i, sem.at[n]))
    for c in writes:
        c.wait()


def third_row(*refs):
    scalars = refs[:4]
    b2, f2, b3, f3, b_here, b_in, b_over, before, out, acc, o_s, sem = refs[4:]
    acc[...] = jnp.zeros_like(acc)
    i = on_parity(scalars, (2, (b2, b3)), (-3, (f3, f2)), (0, 1), (b_here, (b_in, b_over)), acc)
    write_row(o_s, acc, out, i, sem.at[0]).wait()


def last_row(*refs):
    scalars = refs[:4]
    b3, f3, b4, f4, b_here, b_in, b_over, before, out, acc, o_s, sem = refs[4:]
    acc[...] = jnp.zeros_like(acc)
    i = on_parity(scalars, (4, (f4, b4, f3)), (3, (b3, f4, b4)), (0, 1), (b_here, (b_in, b_over)), acc)
    write_row(o_s, acc, out, i, sem.at[0]).wait()


def call(kernel, scalars, held, left, out_shape, scratch, products, alias=False):
    hbm = pl.BlockSpec(memory_space=pl.ANY)
    vmem = pl.BlockSpec(memory_space=pltpu.VMEM)
    return pl.pallas_call(
        kernel,
        out_shape=out_shape,
        grid_spec=pltpu.PrefetchScalarGridSpec(
            num_scalar_prefetch=len(scalars),
            grid=(),
            in_specs=[vmem] * len(held) + [hbm] * len(left),
            out_specs=hbm,
            scratch_shapes=scratch,
        ),
        input_output_aliases={len(scalars) + len(held): 0} if alias else {},
        cost_estimate=pl.CostEstimate(flops=products * 4 * BS**3, bytes_accessed=1 << 20, transcendentals=0),
        compiler_params=pltpu.CompilerParams(vmem_limit_bytes=12 * 1024 * 1024),
    )(*scalars, *held, *left)


CHUNKS = 4


def payload_rows(a_columns, a_live, tile, out, columns, live, wide, rows, sem):
    step = PIECES // CHUNKS
    small = [
        pltpu.make_async_copy(a_columns, columns, sem.at[2 * CHUNKS]),
        pltpu.make_async_copy(a_live, live, sem.at[2 * CHUNKS + 1]),
    ]
    reads = []
    writes = []
    for c in range(CHUNKS):
        part = pl.ds(c * step, step)
        reads.append(pltpu.make_async_copy(tile.at[part], rows.at[part, :PIECE], sem.at[c]))
        writes.append(pltpu.make_async_copy(rows.at[part], out.at[part], sem.at[CHUNKS + c]))
    for c in small + reads:
        c.start()
    wide[...] = jnp.zeros_like(wide)
    for c in small:
        c.wait()
    for s in range(NZA):
        wide[:1, s * MB : (s + 1) * MB] = columns[s].astype(jnp.float32)
    wide[:1, MB * NZA : EACH] = live[...].astype(jnp.float32)
    for p in range(PIECES):
        rows[p, PIECE:, :] = wide[...].astype(jnp.bfloat16)
    for r, w in zip(reads, writes):
        r.wait()
        w.start()
    for w in writes:
        w.wait()


def payload(a_columns, a_live, tile):
    hbm = pl.BlockSpec(memory_space=pltpu.HBM)
    return pl.pallas_call(
        payload_rows,
        out_shape=jax.ShapeDtypeStruct((PIECES, PIECE + META, BS), jnp.bfloat16),
        in_specs=[hbm, hbm, hbm],
        out_specs=hbm,
        scratch_shapes=[
            pltpu.VMEM((NZA, 1, MB), jnp.int32),
            pltpu.VMEM((1, MB), jnp.int32),
            pltpu.VMEM((META, BS), jnp.float32),
            pltpu.VMEM((PIECES, PIECE + META, BS), jnp.bfloat16),
            pltpu.SemaphoreType.DMA((2 * CHUNKS + 2,)),
        ],
        compiler_params=pltpu.CompilerParams(vmem_limit_bytes=4 * 1024 * 1024),
    )(*(pltpu.with_memory_space_constraint(x, pltpu.HBM) for x in (a_columns, a_live, tile)))


def on_device(a_blocks, a_columns, a_live, owner_map, b_blocks, b_columns):
    tile = a_blocks.reshape(PIECES, PIECE, BS)
    cols = lax.axis_size(COL)
    got = lax.all_to_all(payload(a_columns[0].transpose(2, 0, 1), a_live[0], tile), ("z", "y_lo"), 0, 0, tiled=True)
    holder = owner_map[0]
    source = (holder % Z) * Y_LO + holder // Z
    bc_here = b_columns[0, 0]
    bc_next = lax.ppermute(bc_here, COL, col_route(cols)).reshape(-1)
    bc_here = bc_here.reshape(-1)
    place = lax.axis_index("z").astype(jnp.int32)[None]
    b_here = b_blocks[0, 0]
    b_in = lax.ppermute(b_here, COL, within(cols))
    got, bc_here, bc_next, place, b_in = lax.optimization_barrier((got, bc_here, bc_next, place, b_in))

    two = jnp.stack([lax.dynamic_index_in_dim(got, source[k], 0, keepdims=False) for k in range(2)])
    table = two[:, PIECE, :EACH].astype(jnp.int32).reshape(-1)
    own = lax.all_gather(two[:, :PIECE], "y_lo", axis=1, tiled=True)
    b_ready, own, table = lax.optimization_barrier((b_here, own, table))
    b_over = lax.ppermute(b_ready, COL, across(cols))
    ahead = [own]
    back = [own]
    for step in range(3):
        back.append(lax.ppermute(back[-1], "z", z_route(-1)))
        ahead.append(lax.ppermute(ahead[-1], "z", z_route(1)))
    scalars = (place, table, bc_here, bc_next)
    near = (own, back[1], ahead[1], back[2], ahead[2])
    block = (NB, BS, BS)
    shape = jax.ShapeDtypeStruct((MB, BS, NB * BS), jnp.bfloat16)
    b4 = lax.ppermute(back[2][:, SPAN // 2 :], "z", z_route(-2))
    f4 = lax.ppermute(ahead[2][:, : SPAN // 2], "z", z_route(2))
    b_all = (b_here, b_in, b_over)
    wide = [pltpu.VMEM((2,) + block, jnp.float32), pltpu.VMEM((2, BS, NB * BS), jnp.bfloat16), pltpu.SemaphoreType.DMA((2,))]
    slim = [pltpu.VMEM(block, jnp.float32), pltpu.VMEM((BS, NB * BS), jnp.bfloat16), pltpu.SemaphoreType.DMA((1,))]
    window = call(two_rows, scalars, near + b_all, (), shape, wide, 12)
    window = call(third_row, scalars, near[3:] + (back[3], ahead[3]) + b_all, (window,), shape, slim, 6, alias=True)
    window = call(last_row, scalars, (back[3], ahead[3], b4, f4) + b_all, (window,), shape, slim, 6, alias=True)
    return window[None, None]


def solution(mesh):
    fine = Mesh(mesh.devices.reshape(Y_LO, Z, 2, 4, 2), ROW + COL)
    row, col = ROW, COL
    return jax.shard_map(
        on_device,
        mesh=fine,
        in_specs=(
            P(row, col, None, None, None, None),
            P(row, col, None, None),
            P(row, col, None),
            P(col, None),
            P(row, col, None, None, None),
            P(row, col, None, None),
        ),
        out_specs=P(row, col, None, None, None),
        check_vma=False,
    )
```

```python
import jax
import jax.numpy as jnp
from jax import lax
from jax.experimental import pallas as pl
from jax.experimental.pallas import tpu as pltpu
from jax.sharding import Mesh, PartitionSpec as P

BS = 256
MB = 4
NZA = 3
KB = 4
NZB = 2
NB = 4
Y_LO = 4
Z = 8
COL = ("y_hi", "x", "core")
ROW = ("y_lo", "z")
PIECES = Y_LO * Z
PIECE = MB * NZA * BS // PIECES
SPAN = Y_LO * PIECE
META = 8


def z_route(distance):
    return [(i, (i + distance) % Z) for i in range(Z)]


def col_route(n):
    return [((i + 1) % n, i) for i in range(n)]


def within(n):
    return [(a, b) for a, b in col_route(n) if (b + 1) % (n // 2)]


def across(n):
    return [(a, b) for a, b in col_route(n) if not (b + 1) % (n // 2)]


EACH = MB * NZA + MB


def strips(parts):
    found = []
    at = 0
    for ref in parts:
        rows = ref.shape[1]
        off = 0
        while off < rows:
            slot = at // BS
            take = min(rows - off, (slot + 1) * BS - at)
            found.append((slot, at - slot * BS, ref, off, take))
            off += take
            at += take
    return found


def add_products(scalars, i, k, parts, b_ref, acc):
    table, pairs = scalars[1], scalars[2 + k]
    live = table[k * EACH + MB * NZA + i]
    for s in range(NZA):

        @pl.when(s < live)
        def _():
            q = table[k * EACH + s * MB + i]
            b = b_ref[q] if k == 0 else b_ref[0][q] + b_ref[1][q]
            for slot, row, ref, off, take in strips(parts):
                if slot == s:
                    product = jnp.dot(ref[k, off : off + take, :], b, preferred_element_type=jnp.float32)
                    for t in range(NZB):
                        j = pairs[q * NZB + t]
                        acc[j, row : row + take] += product[:, t * BS : (t + 1) * BS]


def on_parity(scalars, even, odd, sections, b_refs, acc):
    z = scalars[0][0]
    for bit, (away, parts) in enumerate((even, odd)):

        @pl.when(z % 2 == bit)
        def _():
            i = ((z + away + Z) % Z) // 2
            for k in sections:
                add_products(scalars, i, k, parts, b_refs[k], acc)

    return ((z + even[0] + (z % 2) * (odd[0] - even[0]) + Z) % Z) // 2


def write_row(o_s, acc, out, i, sem):
    for j in range(NB):
        o_s[:, j * BS : (j + 1) * BS] = acc[j].astype(jnp.bfloat16)
    copy = pltpu.make_async_copy(o_s, out.at[i], sem)
    copy.start()
    return copy


def two_rows(*refs):
    scalars = refs[:4]
    own, b1, f1, b2, f2, b_here, b_in, b_over, out, acc, o_s, sem = refs[4:]
    rows = (((0, (own, b1)), (-1, (f1, own))), ((-2, (f2, f1)), (1, (b1, b2))))
    acc[...] = jnp.zeros_like(acc)
    writes = []
    for n, (even, odd) in enumerate(rows):
        i = on_parity(scalars, even, odd, (0, 1), (b_here, (b_in, b_over)), acc.at[n])
        writes.append(write_row(o_s.at[n], acc.at[n], out, i, sem.at[n]))
    for c in writes:
        c.wait()


def last_rows(*refs):
    scalars = refs[:4]
    b2, f2, b3, f3, b4, f4, b_here, b_in, b_over, before, out, acc, o_s, sem = refs[4:]
    rows = (
        ((2, (b2, b3)), (-3, (f3, f2))),
        ((4, (f4, b4, f3)), (3, (b3, f4, b4))),
    )
    acc[...] = jnp.zeros_like(acc)
    writes = []
    for n, (even, odd) in enumerate(rows):
        i = on_parity(scalars, even, odd, (0, 1), (b_here, (b_in, b_over)), acc.at[n])
        writes.append(write_row(o_s.at[n], acc.at[n], out, i, sem.at[n]))
    for c in writes:
        c.wait()


def call(kernel, scalars, held, left, out_shape, scratch, products, alias=False):
    hbm = pl.BlockSpec(memory_space=pl.ANY)
    vmem = pl.BlockSpec(memory_space=pltpu.VMEM)
    return pl.pallas_call(
        kernel,
        out_shape=out_shape,
        grid_spec=pltpu.PrefetchScalarGridSpec(
            num_scalar_prefetch=len(scalars),
            grid=(),
            in_specs=[vmem] * len(held) + [hbm] * len(left),
            out_specs=hbm,
            scratch_shapes=scratch,
        ),
        input_output_aliases={len(scalars) + len(held): 0} if alias else {},
        cost_estimate=pl.CostEstimate(flops=products * 4 * BS**3, bytes_accessed=1 << 20, transcendentals=0),
        compiler_params=pltpu.CompilerParams(vmem_limit_bytes=12 * 1024 * 1024),
    )(*scalars, *held, *left)


CHUNKS = 4


def payload_rows(a_columns, a_live, tile, out, columns, live, wide, rows, sem):
    step = PIECES // CHUNKS
    small = [
        pltpu.make_async_copy(a_columns, columns, sem.at[2 * CHUNKS]),
        pltpu.make_async_copy(a_live, live, sem.at[2 * CHUNKS + 1]),
    ]
    reads = []
    writes = []
    for c in range(CHUNKS):
        part = pl.ds(c * step, step)
        reads.append(pltpu.make_async_copy(tile.at[part], rows.at[part, :PIECE], sem.at[c]))
        writes.append(pltpu.make_async_copy(rows.at[part], out.at[part], sem.at[CHUNKS + c]))
    for c in small + reads:
        c.start()
    wide[...] = jnp.zeros_like(wide)
    for c in small:
        c.wait()
    for s in range(NZA):
        wide[:1, s * MB : (s + 1) * MB] = columns[s].astype(jnp.float32)
    wide[:1, MB * NZA : EACH] = live[...].astype(jnp.float32)
    for p in range(PIECES):
        rows[p, PIECE:, :] = wide[...].astype(jnp.bfloat16)
    for r, w in zip(reads, writes):
        r.wait()
        w.start()
    for w in writes:
        w.wait()


def payload(a_columns, a_live, tile):
    hbm = pl.BlockSpec(memory_space=pltpu.HBM)
    return pl.pallas_call(
        payload_rows,
        out_shape=jax.ShapeDtypeStruct((PIECES, PIECE + META, BS), jnp.bfloat16),
        in_specs=[hbm, hbm, hbm],
        out_specs=hbm,
        scratch_shapes=[
            pltpu.VMEM((NZA, 1, MB), jnp.int32),
            pltpu.VMEM((1, MB), jnp.int32),
            pltpu.VMEM((META, BS), jnp.float32),
            pltpu.VMEM((PIECES, PIECE + META, BS), jnp.bfloat16),
            pltpu.SemaphoreType.DMA((2 * CHUNKS + 2,)),
        ],
        compiler_params=pltpu.CompilerParams(vmem_limit_bytes=4 * 1024 * 1024),
    )(*(pltpu.with_memory_space_constraint(x, pltpu.HBM) for x in (a_columns, a_live, tile)))


def on_device(a_blocks, a_columns, a_live, owner_map, b_blocks, b_columns):
    tile = a_blocks.reshape(PIECES, PIECE, BS)
    cols = lax.axis_size(COL)
    got = lax.all_to_all(payload(a_columns[0].transpose(2, 0, 1), a_live[0], tile), ("z", "y_lo"), 0, 0, tiled=True)
    holder = owner_map[0]
    source = (holder % Z) * Y_LO + holder // Z
    bc_here = b_columns[0, 0]
    bc_next = lax.ppermute(bc_here, COL, col_route(cols)).reshape(-1)
    bc_here = bc_here.reshape(-1)
    place = lax.axis_index("z").astype(jnp.int32)[None]
    b_here = b_blocks[0, 0]
    b_in = lax.ppermute(b_here, COL, within(cols))
    got, bc_here, bc_next, place, b_in = lax.optimization_barrier((got, bc_here, bc_next, place, b_in))

    two = jnp.stack([lax.dynamic_index_in_dim(got, source[k], 0, keepdims=False) for k in range(2)])
    table = two[:, PIECE, :EACH].astype(jnp.int32).reshape(-1)
    own = lax.all_gather(two[:, :PIECE], "y_lo", axis=1, tiled=True)
    b_ready, own, table = lax.optimization_barrier((b_here, own, table))
    b_over = lax.ppermute(b_ready, COL, across(cols))
    ahead = [own]
    back = [own]
    for step in range(3):
        back.append(lax.ppermute(back[-1], "z", z_route(-1)))
        ahead.append(lax.ppermute(ahead[-1], "z", z_route(1)))
    scalars = (place, table, bc_here, bc_next)
    near = (own, back[1], ahead[1], back[2], ahead[2])
    block = (NB, BS, BS)
    shape = jax.ShapeDtypeStruct((MB, BS, NB * BS), jnp.bfloat16)
    b4 = lax.ppermute(back[2][:, SPAN // 2 :], "z", z_route(-2))
    f4 = lax.ppermute(ahead[2][:, : SPAN // 2], "z", z_route(2))
    b_all = (b_here, b_in, b_over)
    wide = [pltpu.VMEM((2,) + block, jnp.float32), pltpu.VMEM((2, BS, NB * BS), jnp.bfloat16), pltpu.SemaphoreType.DMA((2,))]
    window = call(two_rows, scalars, near + b_all, (), shape, wide, 12)
    far = near[3:] + (back[3], ahead[3], b4, f4)
    window = call(last_rows, scalars, far + b_all, (window,), shape, wide, 12, alias=True)
    return window[None, None]


def solution(mesh):
    fine = Mesh(mesh.devices.reshape(Y_LO, Z, 2, 4, 2), ROW + COL)
    row, col = ROW, COL
    return jax.shard_map(
        on_device,
        mesh=fine,
        in_specs=(
            P(row, col, None, None, None, None),
            P(row, col, None, None),
            P(row, col, None),
            P(col, None),
            P(row, col, None, None, None),
            P(row, col, None, None),
        ),
        out_specs=P(row, col, None, None, None),
        check_vma=False,
    )
```

```python
import jax
import jax.numpy as jnp
from jax import lax
from jax.experimental import pallas as pl
from jax.experimental.pallas import tpu as pltpu
from jax.sharding import Mesh, PartitionSpec as P

BS = 256
MB = 4
NZA = 3
KB = 4
NZB = 2
NB = 4
Y_LO = 4
Z = 8
COL = ("y_hi", "x", "core")
ROW = ("y_lo", "z")
PIECES = Y_LO * Z
PIECE = MB * NZA * BS // PIECES
SPAN = Y_LO * PIECE
META = 8


def z_route(distance):
    return [(i, (i + distance) % Z) for i in range(Z)]


def col_route(n):
    return [((i + 1) % n, i) for i in range(n)]


def within(n):
    return [(a, b) for a, b in col_route(n) if (b + 1) % (n // 2)]


def across(n):
    return [(a, b) for a, b in col_route(n) if not (b + 1) % (n // 2)]


EACH = MB * NZA + MB


def strips(parts):
    found = []
    at = 0
    for ref in parts:
        rows = ref.shape[1]
        off = 0
        while off < rows:
            slot = at // BS
            take = min(rows - off, (slot + 1) * BS - at)
            found.append((slot, at - slot * BS, ref, off, take))
            off += take
            at += take
    return found


def add_products(scalars, i, k, parts, b_ref, acc):
    table, pairs = scalars[1], scalars[2 + k]
    live = table[k * EACH + MB * NZA + i]
    for s in range(NZA):

        @pl.when(s < live)
        def _():
            q = table[k * EACH + s * MB + i]
            b = b_ref[q] if k == 0 else b_ref[0][q] + b_ref[1][q]
            for slot, row, ref, off, take in strips(parts):
                if slot == s:
                    product = jnp.dot(ref[k, off : off + take, :], b, preferred_element_type=jnp.float32)
                    for t in range(NZB):
                        j = pairs[q * NZB + t]
                        acc[j, row : row + take] += product[:, t * BS : (t + 1) * BS]


def on_parity(scalars, even, odd, sections, b_refs, acc):
    z = scalars[0][0]
    for bit, (away, parts) in enumerate((even, odd)):

        @pl.when(z % 2 == bit)
        def _():
            i = ((z + away + Z) % Z) // 2
            for k in sections:
                add_products(scalars, i, k, parts, b_refs[k], acc)

    return ((z + even[0] + (z % 2) * (odd[0] - even[0]) + Z) % Z) // 2


def write_row(o_s, acc, out, i, sem):
    for j in range(NB):
        o_s[:, j * BS : (j + 1) * BS] = acc[j].astype(jnp.bfloat16)
    copy = pltpu.make_async_copy(o_s, out.at[i], sem)
    copy.start()
    return copy


def two_rows(*refs):
    scalars = refs[:4]
    own, b1, f1, b2, f2, b_here, b_in, b_over, out, acc, o_s, sem = refs[4:]
    rows = (((0, (own, b1)), (-1, (f1, own))), ((-2, (f2, f1)), (1, (b1, b2))))
    acc[...] = jnp.zeros_like(acc)
    writes = []
    for n, (even, odd) in enumerate(rows):
        i = on_parity(scalars, even, odd, (0, 1), (b_here, (b_in, b_over)), acc.at[n])
        writes.append(write_row(o_s.at[n], acc.at[n], out, i, sem.at[n]))
    for c in writes:
        c.wait()


def last_rows(*refs):
    scalars = refs[:4]
    f2, b2, f3, b3, f4, b4, b_here, b_in, b_over, before, out, acc, o_s, sem = refs[4:]
    rows = (
        ((2, (b2, b3)), (-3, (f3, f2))),
        ((4, (f4, b4, f3)), (3, (b3, f4, b4))),
    )
    acc[...] = jnp.zeros_like(acc)
    writes = []
    for n, (even, odd) in enumerate(rows):
        i = on_parity(scalars, even, odd, (0, 1), (b_here, (b_in, b_over)), acc.at[n])
        writes.append(write_row(o_s.at[n], acc.at[n], out, i, sem.at[n]))
    for c in writes:
        c.wait()


def call(kernel, scalars, held, left, out_shape, scratch, products, alias=False):
    hbm = pl.BlockSpec(memory_space=pl.ANY)
    vmem = pl.BlockSpec(memory_space=pltpu.VMEM)
    return pl.pallas_call(
        kernel,
        out_shape=out_shape,
        grid_spec=pltpu.PrefetchScalarGridSpec(
            num_scalar_prefetch=len(scalars),
            grid=(),
            in_specs=[vmem] * len(held) + [hbm] * len(left),
            out_specs=hbm,
            scratch_shapes=scratch,
        ),
        input_output_aliases={len(scalars) + len(held): 0} if alias else {},
        cost_estimate=pl.CostEstimate(flops=products * 4 * BS**3, bytes_accessed=1 << 20, transcendentals=0),
        compiler_params=pltpu.CompilerParams(vmem_limit_bytes=12 * 1024 * 1024),
    )(*scalars, *held, *left)


CHUNKS = 4


def payload_rows(a_columns, a_live, tile, out, columns, live, wide, rows, sem):
    step = PIECES // CHUNKS
    small = [
        pltpu.make_async_copy(a_columns, columns, sem.at[2 * CHUNKS]),
        pltpu.make_async_copy(a_live, live, sem.at[2 * CHUNKS + 1]),
    ]
    reads = []
    writes = []
    for c in range(CHUNKS):
        part = pl.ds(c * step, step)
        reads.append(pltpu.make_async_copy(tile.at[part], rows.at[part, :PIECE], sem.at[c]))
        writes.append(pltpu.make_async_copy(rows.at[part], out.at[part], sem.at[CHUNKS + c]))
    for c in small + reads:
        c.start()
    wide[...] = jnp.zeros_like(wide)
    for c in small:
        c.wait()
    for s in range(NZA):
        wide[:1, s * MB : (s + 1) * MB] = columns[s].astype(jnp.float32)
    wide[:1, MB * NZA : EACH] = live[...].astype(jnp.float32)
    for p in range(PIECES):
        rows[p, PIECE:, :] = wide[...].astype(jnp.bfloat16)
    for r, w in zip(reads, writes):
        r.wait()
        w.start()
    for w in writes:
        w.wait()


def payload(a_columns, a_live, tile):
    hbm = pl.BlockSpec(memory_space=pltpu.HBM)
    return pl.pallas_call(
        payload_rows,
        out_shape=jax.ShapeDtypeStruct((PIECES, PIECE + META, BS), jnp.bfloat16),
        in_specs=[hbm, hbm, hbm],
        out_specs=hbm,
        scratch_shapes=[
            pltpu.VMEM((NZA, 1, MB), jnp.int32),
            pltpu.VMEM((1, MB), jnp.int32),
            pltpu.VMEM((META, BS), jnp.float32),
            pltpu.VMEM((PIECES, PIECE + META, BS), jnp.bfloat16),
            pltpu.SemaphoreType.DMA((2 * CHUNKS + 2,)),
        ],
        compiler_params=pltpu.CompilerParams(vmem_limit_bytes=4 * 1024 * 1024),
    )(*(pltpu.with_memory_space_constraint(x, pltpu.HBM) for x in (a_columns, a_live, tile)))


def on_device(a_blocks, a_columns, a_live, owner_map, b_blocks, b_columns):
    tile = a_blocks.reshape(PIECES, PIECE, BS)
    cols = lax.axis_size(COL)
    got = lax.all_to_all(payload(a_columns[0].transpose(2, 0, 1), a_live[0], tile), ("z", "y_lo"), 0, 0, tiled=True)
    holder = owner_map[0]
    source = (holder % Z) * Y_LO + holder // Z
    bc_here = b_columns[0, 0]
    bc_next = lax.ppermute(bc_here, COL, col_route(cols)).reshape(-1)
    bc_here = bc_here.reshape(-1)
    place = lax.axis_index("z").astype(jnp.int32)[None]
    b_here = b_blocks[0, 0]
    b_in = lax.ppermute(b_here, COL, within(cols))
    got, bc_here, bc_next, place, b_in = lax.optimization_barrier((got, bc_here, bc_next, place, b_in))

    two = jnp.stack([lax.dynamic_index_in_dim(got, source[k], 0, keepdims=False) for k in range(2)])
    table = two[:, PIECE, :EACH].astype(jnp.int32).reshape(-1)
    own = lax.all_gather(two[:, :PIECE], "y_lo", axis=1, tiled=True)
    b_ready, own, table = lax.optimization_barrier((b_here, own, table))
    b_over = lax.ppermute(b_ready, COL, across(cols))
    ahead = [own]
    back = [own]
    for step in range(3):
        back.append(lax.ppermute(back[-1], "z", z_route(-1)))
        ahead.append(lax.ppermute(ahead[-1], "z", z_route(1)))
    scalars = (place, table, bc_here, bc_next)
    near = (own, back[1], ahead[1], back[2], ahead[2])
    block = (NB, BS, BS)
    shape = jax.ShapeDtypeStruct((MB, BS, NB * BS), jnp.bfloat16)
    b4 = lax.ppermute(back[2][:, SPAN // 2 :], "z", z_route(-2))
    f4 = lax.ppermute(ahead[2][:, : SPAN // 2], "z", z_route(2))
    b_all = (b_here, b_in, b_over)
    wide = [pltpu.VMEM((2,) + block, jnp.float32), pltpu.VMEM((2, BS, NB * BS), jnp.bfloat16), pltpu.SemaphoreType.DMA((2,))]
    window = call(two_rows, scalars, near + b_all, (), shape, wide, 12)
    far = (ahead[2], back[2], ahead[3], back[3], f4, b4)
    window = call(last_rows, scalars, far + b_all, (window,), shape, wide, 12, alias=True)
    return window[None, None]


def solution(mesh):
    fine = Mesh(mesh.devices.reshape(Y_LO, Z, 2, 4, 2), ROW + COL)
    row, col = ROW, COL
    return jax.shard_map(
        on_device,
        mesh=fine,
        in_specs=(
            P(row, col, None, None, None, None),
            P(row, col, None, None),
            P(row, col, None),
            P(col, None),
            P(row, col, None, None, None),
            P(row, col, None, None),
        ),
        out_specs=P(row, col, None, None, None),
        check_vma=False,
    )
```
